256 devices in a mesh: tm: 64 (over z_lo, y, x), space: 4 (over z_hi, core).
Axes of the slice: x: 4, y: 4, z: 8 (z_hi: 2, z_lo: 4; z = z_hi * 4 + z_lo), core: 2. Of those that a mesh axis runs over, the one named last changes fastest.
Arguments:
- state_field: float32 [128, 16, 16, 128], P('tm', 'space'), may hold values from -3 to 3
- adjoint: float32 [128, 16, 16, 128], P('tm', 'space'), may hold values from -3 to 3
- target: float32 [128, 16, 16, 128], P('tm', 'space'), may hold values from -4 to 4
- initial_state: float32 [16, 16, 128], P('space'), may hold values from -4 to 4
- conductivity: float32 [16, 16, 128], P('space'), may hold values from 0.05 to 0.5
- reaction: float32 [16, 16, 128], P('space'), may hold values from 0.05 to 1
Outputs:
- new_state: float32 [128, 16, 16, 128], P('tm', 'space')
- new_adjoint: float32 [128, 16, 16, 128], P('tm', 'space')
The draws below stay inside these ranges and needn't reach their ends.
All inputs are finite; a program needn't handle non-finite values.
Results may differ from the reference program's by a relative error of at most 0.00029.
Values sent between devices are 32-bit elements; how exact they have to be, the bound alone decides.
No kernel may reach another device: no remote copies, remote signals or barrier semaphores. Data moves between devices by JAX's collectives and lax.ppermute only.
A program may use at most 64 MiB of HBM per device.

```python
import math
import jax
import jax.numpy as jnp
from jax import lax

NY = 16
NZ = 128
CHEB = 8
NT = 128
NX = 16


def block_levels(rng, extent, pieces, low, largest):
    loudness, own = 1.0, jax.random.fold_in(rng, 6)
    for position, blocks in pieces:
        steps = jnp.exp(jax.random.uniform(jax.random.fold_in(own, position), (blocks,), jnp.float32, low / len(pieces), largest / len(pieces)))
        loudness = loudness * jnp.repeat(steps, extent[position] // blocks).reshape([-1 if axis == position else 1 for axis in range(len(extent))])
    return loudness


def bell_draw(own_key, shape, width, limit, pieces=(), kind=jnp.bfloat16):
    entries = jax.random.normal(own_key, shape, jnp.float32) * width
    if len(pieces) > 0:
        entries = block_levels(own_key, shape, pieces, -0.22, 0.18) * entries
    return jnp.clip(entries, min=-limit, max=limit).astype(kind)


def setup_inputs(seed: int = 0) -> dict:
    keys = jax.random.split(jax.random.key(seed), 7)
    state_field = bell_draw(keys[0], (NT, NX, NY, NZ), 0.5, 3.0, ((0, 64), (1, 4)), jnp.float32)
    adjoint = bell_draw(keys[1], (NT, NX, NY, NZ), 0.5, 3.0, ((0, 64), (1, 4)), jnp.float32)
    target = bell_draw(keys[2], (NT, NX, NY, NZ), 1.0, 4.0, ((0, 64), (1, 4)), jnp.float32)
    initial_state = bell_draw(keys[3], (NX, NY, NZ), 1.0, 4.0, ((0, 4),), jnp.float32)
    conductivity = jnp.clip(jnp.exp(math.log(0.5) - 2.3025851 * jax.random.uniform(keys[4], (NX, NY, NZ), jnp.float32) ** block_levels(keys[4], (NX, NY, NZ), ((0, 4),), -0.2, 0.2)), 0.05, 0.5)
    reaction = jnp.clip(jnp.exp(math.log(1.0) - 2.9957323 * jax.random.uniform(keys[5], (NX, NY, NZ), jnp.float32) ** block_levels(keys[5], (NX, NY, NZ), ((0, 4),), -0.2, 0.2)), 0.05, 1.0)
    return dict(state_field=state_field, adjoint=adjoint, target=target, initial_state=initial_state, conductivity=conductivity, reaction=reaction)


highest = lax.Precision.HIGHEST
step_rate = 2.0
coupling = 1.0
lower_edge = 0.05
upper_edge = 7.0


def diffusion(padded, cond_pad):
    centre = padded[..., 1:-1, :, :]
    cond_mid = cond_pad[1:-1]
    result = (0.5 * (cond_mid + cond_pad[2:])) * (centre - padded[..., 2:, :, :])
    result = result + (0.5 * (cond_mid + cond_pad[:-2])) * (centre - padded[..., :-2, :, :])
    value_pad = jnp.pad(centre, [(0, 0)] * (centre.ndim - 2) + [(1, 1), (1, 1)])
    cond_side = jnp.pad(cond_mid, ((0, 0), (1, 1), (1, 1)))
    neighbours = ((value_pad[..., 2:, 1:-1], cond_side[:, 2:, 1:-1]),
                  (value_pad[..., :-2, 1:-1], cond_side[:, :-2, 1:-1]),
                  (value_pad[..., 1:-1, 2:], cond_side[:, 1:-1, 2:]),
                  (value_pad[..., 1:-1, :-2], cond_side[:, 1:-1, :-2]))
    for side_value, side_cond in neighbours:
        result = result + (0.5 * (cond_mid + side_cond)) * (centre - side_value)
    return result


def unit_circle_arguments(mode_number, temporal_nodes, accumulated_sum):
    return (2.0 * math.pi / accumulated_sum) * ((mode_number * temporal_nodes) % accumulated_sum).astype(jnp.float32)


def chebyshev(right_side, apply_system, lower_bound, upper_bound):
    centre_value = 0.5 * (upper_bound + lower_bound)
    half_width = 0.5 * (upper_bound - lower_bound)
    ratio_value = centre_value / half_width
    rho_now = 1.0 / ratio_value
    solution = jnp.zeros_like(right_side)
    residue = right_side
    direction = right_side / centre_value
    for repeat in range(CHEB):
        solution = solution + direction
        if repeat + 1 < CHEB:
            residue = residue - apply_system(direction)
            rho_next = 1.0 / (2.0 * ratio_value - rho_now)
            direction = (rho_next * rho_now) * direction + (2.0 * rho_next / half_width) * residue
            rho_now = rho_next
    return solution


def reference(state_field, adjoint, target, initial_state, conductivity, reaction):
    horizon_length = state_field.shape[0]
    grid_shape = state_field.shape[1:]
    cell_count = grid_shape[0] * grid_shape[1] * grid_shape[2]
    x_pad = ((0, 0), (1, 1), (0, 0), (0, 0))
    cond_pad = jnp.pad(conductivity, ((1, 1), (0, 0), (0, 0)))
    preceding_iterate = jnp.concatenate([initial_state[None], state_field[:-1]], 0)
    later_steps = jnp.concatenate([adjoint[1:], jnp.zeros_like(adjoint[:1])], 0)
    diff_state = diffusion(jnp.pad(state_field, x_pad), cond_pad)
    diff_adjoint = diffusion(jnp.pad(adjoint, x_pad), cond_pad)
    state_res = step_rate * (state_field - preceding_iterate) + diff_state + state_field * state_field * state_field / 3.0 + coupling * adjoint
    adjoint_res = step_rate * (adjoint - later_steps) + diff_adjoint + state_field * state_field * adjoint - state_field + target
    residual = jnp.stack([state_res, adjoint_res]).reshape(2, horizon_length, cell_count)
    mode_number = jnp.arange(horizon_length, dtype=jnp.int32)[:, None]
    temporal_nodes = jnp.arange(horizon_length, dtype=jnp.int32)[None, :]
    diagonal_twist_weights = unit_circle_arguments(mode_number, temporal_nodes, horizon_length)
    cosine_table = jnp.cos(diagonal_twist_weights)
    sine_table = jnp.sin(diagonal_twist_weights)
    forward = jnp.stack([cosine_table, -sine_table])
    spectral = jnp.einsum("rkt,ftc->kfrc", forward, residual, precision=highest)
    block_size = math.gcd(horizon_length, 16)
    blocks = spectral.reshape((horizon_length // block_size, block_size, 2, 2) + grid_shape)
    thetas = unit_circle_arguments(jnp.arange(horizon_length, dtype=jnp.int32), 1, horizon_length)
    shift_all = (step_rate * (1.0 - jnp.cos(thetas))).reshape(horizon_length // block_size, block_size)
    twist_all = (step_rate * jnp.sin(thetas)).reshape(horizon_length // block_size, block_size)

    def solve_block(operands):
        fields, shift_block, twist_block = operands
        shifts = shift_block.reshape(-1, 1, 1, 1, 1, 1)
        spread = (twist_block * twist_block + coupling).reshape(-1, 1, 1, 1, 1, 1)
        lower_bound = (lower_edge + shifts) ** 2 + spread
        upper_bound = (upper_edge + shifts) ** 2 + spread

        def shifted(field):
            padded = jnp.pad(field, [(0, 0)] * 3 + [(1, 1), (0, 0), (0, 0)])
            return diffusion(padded, cond_pad) + (reaction + shifts) * field

        def apply_system(field):
            return shifted(shifted(field)) + spread * field

        solved = chebyshev(fields, apply_system, lower_bound, upper_bound)
        operator_output = shifted(solved)
        twists = twist_block.reshape(-1, 1, 1, 1)
        first_real = solved[:, 0, 0]
        first_imag = solved[:, 0, 1]
        second_real = solved[:, 1, 0]
        second_imag = solved[:, 1, 1]
        twisted = jnp.stack([
            jnp.stack([-twists * first_imag + coupling * second_real, twists * first_real + coupling * second_imag], 1),
            jnp.stack([-first_real + twists * second_imag, -first_imag - twists * second_real], 1)], 1)
        return operator_output - twisted

    corrected = lax.map(solve_block, (blocks, shift_all, twist_all))
    corrected = corrected.reshape(horizon_length, 2, 2, cell_count)
    inverse = forward / horizon_length
    delta_steps = jnp.einsum("rkt,kfrc->ftc", inverse, corrected, precision=highest)
    delta_steps = delta_steps.reshape((2, horizon_length) + grid_shape)
    return state_field - delta_steps[0], adjoint - delta_steps[1]
```

```python
import functools

import jax
import jax.numpy as jnp
import numpy as np
from jax import lax
from jax.experimental import pallas as pl
from jax.experimental.pallas import tpu as pltpu
from jax.sharding import PartitionSpec as P

CHEB = 8
step_rate = 2.0
coupling = 1.0
lower_edge = 0.05
upper_edge = 7.0
COEF = 32
vmem = functools.partial(pl.BlockSpec, memory_space=pltpu.VMEM)
grant = pltpu.CompilerParams(vmem_limit_bytes=8 * 1024 * 1024)
smem = functools.partial(pl.BlockSpec, memory_space=pltpu.SMEM)


def time_tables(horizon, slots):
    k = np.arange(slots)[:, None]
    n = np.concatenate([np.arange(0, horizon, 2), np.arange(1, horizon, 2)])[None, :]
    angle = 2.0 * np.pi / horizon * ((k * n) % horizon)
    cosine, sine = np.cos(angle), np.sin(angle)
    alternation = np.where(n % 2 == 0, 1.0, -1.0)
    forward = np.concatenate([cosine, np.where(k == 0, alternation, -sine)], 0)
    inverse = (
        np.concatenate(
            [
                np.where(k == 0, 1.0, 2.0) * cosine,
                np.where(k == 0, alternation, -2.0 * sine),
            ],
            0,
        )
        / horizon
    )
    return forward.astype(np.float32), inverse.T.astype(np.float32)


def solver_table(horizon, slots):
    theta = 2.0 * np.pi / horizon * np.arange(slots + 1)
    shift = step_rate * (1.0 - np.cos(theta))
    twist = step_rate * np.sin(theta)
    twist[slots] = 0.0
    spread = twist * twist + coupling
    lower = (lower_edge + shift) ** 2 + spread
    upper = (upper_edge + shift) ** 2 + spread
    centre = 0.5 * (upper + lower)
    half = 0.5 * (upper - lower)
    ratio = centre / half
    rho = 1.0 / ratio
    table = np.zeros((slots + 1, COEF))
    table[:, 0] = shift
    table[:, 1] = spread
    table[:, 2] = 1.0 / centre
    for step in range(CHEB - 1):
        rho_next = 1.0 / (2.0 * ratio - rho)
        table[:, 4 + 2 * step] = rho_next * rho
        table[:, 5 + 2 * step] = 2.0 * rho_next / half
        rho = rho_next
    return table.reshape(-1).astype(np.float32), twist[:slots]


def pack_kernel(y_ref, p_ref, t_ref, c_ref, r_ref, o_ref, m_ref):
    m_ref[0] = c_ref[...]
    m_ref[1] = r_ref[...]
    for j in range(2):
        y = y_ref[j]
        p = p_ref[j]
        square = y * y
        o_ref[:, j, :] = y
        o_ref[:, 2 + j, :] = p
        o_ref[:, 4 + j, :] = square * y * (1.0 / 3.0) + coupling * p
        o_ref[:, 6 + j, :] = square * p - y + t_ref[j]


def forward_kernel(f_ref, init_ref, x_ref, o_ref):
    rows = x_ref.shape[0]
    lanes = x_ref.shape[2]
    mine = lax.axis_index("tm")
    y0, y1, p0, p1, g0, g1, h0, h1 = (x_ref[:, i, :] for i in range(8))
    row = lax.broadcasted_iota(jnp.int32, (rows, lanes), 0)
    before = jnp.where(row == 0, init_ref[pl.ds(mine, 1), :], pltpu.roll(y1, 1, 0))
    after = jnp.where(row == rows - 1, 0.0, pltpu.roll(p0, rows - 1, 0))
    a0 = g0 + step_rate * (y0 - before)
    a1 = g1 + step_rate * (y1 - y0)
    b0 = h0 + step_rate * (p0 - p1)
    b1 = h1 + step_rate * (p1 - after)
    data = jnp.concatenate(
        [
            jnp.concatenate([a0, b0, y0, p0], 1),
            jnp.concatenate([a1, b1, y1, p1], 1),
        ],
        0,
    )
    hat = lax.dot(
        f_ref[...], data, precision=lax.Precision.HIGHEST, preferred_element_type=jnp.float32
    )
    for f in range(2):
        for r in range(2):
            for q in range(2):
                column = (q * 2 + f) * lanes
                o_ref[:, (f * 2 + r) * 2 + q, :] = hat[
                    r * rows : (r + 1) * rows, column : column + lanes
                ]


def solve_kernel(
    co_ref,
    m0_ref,
    m1_ref,
    m2_ref,
    m3_ref,
    x_ref,
    o_ref,
    mat,
    cx,
    cyp,
    cym,
    czp,
    czm,
    diag,
    yy,
    res,
    d,
    t,
    w,
):
    slot = lax.axis_index("tm")
    item = lax.axis_index("space")
    slots = x_ref.shape[0]
    frequency = jnp.where((slot == 0) & (item % 2 == 1), slots, slot)
    base = frequency * COEF
    shift = co_ref[base]
    spread = co_ref[base + 1]
    start = co_ref[base + 2]
    for piece, ref in enumerate((m0_ref, m1_ref, m2_ref, m3_ref)):
        mat[item ^ piece] = ref[...]
    slabs = 4
    width = mat.shape[2]
    count_y, lanes = mat.shape[3], mat.shape[4]
    count = slabs * width
    row = lax.broadcasted_iota(jnp.int32, (count_y, lanes), 0)
    lane = lax.broadcasted_iota(jnp.int32, (count_y, lanes), 1)

    def cond(x):
        return mat[x // width, 0, x % width]

    for x in range(count):
        c = cond(x)
        half = 0.5 * c
        total = mat[x // width, 1, x % width] + shift
        up = 0.5 * (c + cond(x + 1)) if x + 1 < count else half
        down = 0.5 * (c + cond(x - 1)) if x > 0 else half
        if x + 1 < count:
            cx[x] = up
        yp = jnp.where(row == count_y - 1, 0.0, 0.5 * pltpu.roll(c, count_y - 1, 0)) + half
        ym = jnp.where(row == 0, 0.0, 0.5 * pltpu.roll(c, 1, 0)) + half
        zp = jnp.where(lane == lanes - 1, 0.0, 0.5 * pltpu.roll(c, lanes - 1, 1)) + half
        zm = jnp.where(lane == 0, 0.0, 0.5 * pltpu.roll(c, 1, 1)) + half
        diag[x] = (up + down) + (yp + ym) + (zp + zm) + total
        cyp[x] = jnp.where(row == count_y - 1, 0.0, yp)
        cym[x] = jnp.where(row == 0, 0.0, ym)
        czp[x] = jnp.where(lane == lanes - 1, 0.0, zp)
        czm[x] = jnp.where(lane == 0, 0.0, zm)
    for s in range(slabs):
        res[s * width : (s + 1) * width] = x_ref[:, 2 * s, :].reshape(width, count_y, lanes)
        yy[s * width : (s + 1) * width] = x_ref[:, 2 * s + 1, :].reshape(width, count_y, lanes)

    def applied(ref, x):
        v = ref[x]
        out = diag[x] * v
        if x + 1 < count:
            out = out - cx[x] * ref[x + 1]
        if x > 0:
            out = out - cx[x - 1] * ref[x - 1]
        out = out - cyp[x] * pltpu.roll(v, count_y - 1, 0)
        out = out - cym[x] * pltpu.roll(v, 1, 0)
        out = out - czp[x] * pltpu.roll(v, lanes - 1, 1)
        out = out - czm[x] * pltpu.roll(v, 1, 1)
        return v, out

    for x in range(count):
        v, out = applied(yy, x)
        r = res[x] + out - (mat[x // width, 1, x % width] + shift) * v
        first = start * r
        res[x] = r
        d[x] = first
        w[x] = first

    def step(i, carry):
        alpha = co_ref[base + 4 + 2 * i]
        beta = co_ref[base + 5 + 2 * i]
        for x in range(count):
            t[x] = applied(d, x)[1]
        for x in range(count):
            now = d[x]
            r = res[x] - (applied(t, x)[1] + spread * now)
            now = alpha * now + beta * r
            res[x] = r
            d[x] = now
            w[x] = w[x] + now
        return carry

    lax.fori_loop(0, CHEB - 1, step, 0)
    for x in range(count):
        t[x] = applied(w, x)[1]
    for s in range(slabs):
        o_ref[:, 2 * s, :] = w[s * width : (s + 1) * width].reshape(width * count_y, lanes)
        o_ref[:, 2 * s + 1, :] = t[s * width : (s + 1) * width].reshape(width * count_y, lanes)


def inverse_kernel(g_ref, b_ref, x_ref, o_ref):
    rows = x_ref.shape[0]
    lanes = x_ref.shape[2]
    b = b_ref[...]
    u_re, ku_re, u_im, ku_im, v_re, kv_re, v_im, kv_im = (x_ref[:, i, :] for i in range(8))
    c00 = ku_re - (coupling * v_re - b * u_im)
    c01 = ku_im - (coupling * v_im + b * u_re)
    c10 = kv_re - (b * v_im - u_re)
    c11 = kv_im + (b * v_re + u_im)
    data = jnp.concatenate(
        [jnp.concatenate([c00, c10], 1), jnp.concatenate([c01, c11], 1)],
        0,
    )
    back = lax.dot(
        g_ref[...], data, precision=lax.Precision.HIGHEST, preferred_element_type=jnp.float32
    )
    for f in range(2):
        for j in range(2):
            o_ref[:, f * 2 + j, :] = back[
                j * rows : (j + 1) * rows, f * lanes : (f + 1) * lanes
            ]


def update_kernel(y_ref, p_ref, d_ref, ny_ref, np_ref):
    for j in range(2):
        ny_ref[j] = y_ref[j] - d_ref[:, j, :]
        np_ref[j] = p_ref[j] - d_ref[:, 2 + j, :]


def swapped(value, distance):
    count = lax.axis_size("space")
    return lax.ppermute(value, "space", [(i, i ^ distance) for i in range(count)])


def shards(state_field, adjoint, target, initial_state, conductivity, reaction):
    steps, width_x, width_y, width_z = state_field.shape
    devices = lax.axis_size("tm")
    spaces = lax.axis_size("space")
    rows = width_x * width_y
    horizon = steps * devices
    assert steps == 2 and rows == devices and spaces == 4
    f32 = jnp.float32

    def shape(*dims):
        return jax.ShapeDtypeStruct(dims, f32)

    flat = (steps, rows, width_z)
    state_rows = state_field.reshape(flat)
    adjoint_rows = adjoint.reshape(flat)
    packed, material = pl.pallas_call(
        pack_kernel,
        out_shape=(
            shape(rows, 8, width_z),
            shape(2, width_x, width_y, width_z),
        ),
        in_specs=[vmem()] * 5,
        out_specs=(vmem(), vmem()),
        compiler_params=grant,
        name="pack",
    )(state_rows, adjoint_rows, target.reshape(flat), conductivity, reaction)
    material_core = swapped(material, 1)
    material_far = swapped(material, 2)
    material_both = swapped(material, 3)
    forward, inverse = time_tables(horizon, devices)
    table, twist = solver_table(horizon, devices)
    by_cell = lax.all_to_all(packed, "tm", 0, 0, tiled=True)
    hat = pl.pallas_call(
        forward_kernel,
        out_shape=shape(devices, 8, width_z),
        in_specs=[vmem()] * 3,
        out_specs=vmem(),
        compiler_params=grant,
        name="forward",
    )(jnp.asarray(forward), initial_state.reshape(rows, width_z), by_cell)
    everyone = ("tm", "space")
    pairs = (devices * spaces, 2, width_z)
    by_item = lax.all_to_all(hat.reshape(pairs), everyone, 0, 0, tiled=True)
    grid = (spaces * width_x, width_y, width_z)
    solved = pl.pallas_call(
        solve_kernel,
        out_shape=shape(rows, 8, width_z),
        in_specs=[smem()] + [vmem()] * 5,
        out_specs=vmem(),
        scratch_shapes=[pltpu.VMEM((spaces, 2, width_x, width_y, width_z), f32)]
        + [pltpu.VMEM(grid, f32)] * 11,
        compiler_params=grant,
        name="solve",
    )(
        jnp.asarray(table),
        material,
        material_core,
        material_far,
        material_both,
        by_item.reshape(rows, 8, width_z),
    )
    by_row = lax.all_to_all(solved.reshape(pairs), everyone, 0, 0, tiled=True)
    twists = np.broadcast_to(twist.astype(np.float32)[:, None], (devices, width_z))
    delta = pl.pallas_call(
        inverse_kernel,
        out_shape=shape(devices, 4, width_z),
        in_specs=[vmem()] * 3,
        out_specs=vmem(),
        compiler_params=grant,
        name="inverse",
    )(jnp.asarray(inverse), jnp.asarray(twists), by_row.reshape(devices, 8, width_z))
    by_time = lax.all_to_all(delta, "tm", 0, 0, tiled=True)
    new_state, new_adjoint = pl.pallas_call(
        update_kernel,
        out_shape=(shape(*flat), shape(*flat)),
        in_specs=[vmem()] * 3,
        out_specs=(vmem(), vmem()),
        compiler_params=grant,
        name="update",
    )(state_rows, adjoint_rows, by_time)
    return new_state.reshape(state_field.shape), new_adjoint.reshape(adjoint.shape)


def solution(mesh):
    in_specs = (
        P("tm", "space", None, None),
        P("tm", "space", None, None),
        P("tm", "space", None, None),
        P("space", None, None),
        P("space", None, None),
        P("space", None, None),
    )
    out_specs = (P("tm", "space", None, None), P("tm", "space", None, None))
    return jax.shard_map(shards, mesh=mesh, in_specs=in_specs, out_specs=out_specs, check_vma=False)
```

```python
import functools

import jax
import jax.numpy as jnp
import numpy as np
from jax import lax
from jax.experimental import pallas as pl
from jax.experimental.pallas import tpu as pltpu
from jax.sharding import PartitionSpec as P

CHEB = 8
step_rate = 2.0
coupling = 1.0
lower_edge = 0.05
upper_edge = 7.0
COEF = 32
vmem = functools.partial(pl.BlockSpec, memory_space=pltpu.VMEM)
grant = pltpu.CompilerParams(vmem_limit_bytes=8 * 1024 * 1024)
hbm = functools.partial(pl.BlockSpec, memory_space=pltpu.HBM)
smem = functools.partial(pl.BlockSpec, memory_space=pltpu.SMEM)


def time_tables(horizon, slots):
    k = np.arange(slots)[:, None]
    n = np.concatenate([np.arange(0, horizon, 2), np.arange(1, horizon, 2)])[None, :]
    angle = 2.0 * np.pi / horizon * ((k * n) % horizon)
    cosine, sine = np.cos(angle), np.sin(angle)
    alternation = np.where(n % 2 == 0, 1.0, -1.0)
    forward = np.concatenate([cosine, np.where(k == 0, alternation, -sine)], 0)
    inverse = (
        np.concatenate(
            [
                np.where(k == 0, 1.0, 2.0) * cosine,
                np.where(k == 0, alternation, -2.0 * sine),
            ],
            0,
        )
        / horizon
    )
    return forward.astype(np.float32), inverse.T.astype(np.float32)


def solver_table(horizon, slots):
    theta = 2.0 * np.pi / horizon * np.arange(slots + 1)
    shift = step_rate * (1.0 - np.cos(theta))
    twist = step_rate * np.sin(theta)
    twist[slots] = 0.0
    spread = twist * twist + coupling
    lower = (lower_edge + shift) ** 2 + spread
    upper = (upper_edge + shift) ** 2 + spread
    centre = 0.5 * (upper + lower)
    half = 0.5 * (upper - lower)
    ratio = centre / half
    rho = 1.0 / ratio
    table = np.zeros((slots + 1, COEF))
    table[:, 0] = shift
    table[:, 1] = spread
    table[:, 2] = 1.0 / centre
    for step in range(CHEB - 1):
        rho_next = 1.0 / (2.0 * ratio - rho)
        table[:, 4 + 2 * step] = rho_next * rho
        table[:, 5 + 2 * step] = 2.0 * rho_next / half
        rho = rho_next
    return table.reshape(-1).astype(np.float32), twist[:slots]


def twist_block(twist):
    block = np.zeros((twist.shape[0], 128), np.float32)
    block[:, 0] = twist
    return block


def rows_of(count, start, stride):
    return pl.ds(start, count, stride=stride)


def pack_kernel(c_hbm, r_hbm, y_hbm, p_hbm, t_hbm, o_ref, m_ref, y_ref, p_ref, t_ref, sem):
    copies = [
        pltpu.make_async_copy(source, target, sem.at[i])
        for i, (source, target) in enumerate(
            (
                (y_hbm, y_ref),
                (p_hbm, p_ref),
                (t_hbm, t_ref),
                (c_hbm, m_ref.at[0]),
                (r_hbm, m_ref.at[1]),
            )
        )
    ]
    for copy in copies:
        copy.start()
    for copy in copies:
        copy.wait()
    rows = y_ref.shape[1]
    for i, ref in enumerate((y_ref, p_ref, t_ref)):
        for j in range(2):
            o_ref[rows_of(rows, 2 * i + j, 6), :] = ref[j]


def halves(value):
    high = value.astype(jnp.bfloat16)
    return high, (value - high.astype(jnp.float32)).astype(jnp.bfloat16)


def product(high, low, data):
    data_high, data_low = halves(data)
    dot = functools.partial(lax.dot, preferred_element_type=jnp.float32)
    return dot(high, data_high) + (dot(high, data_low) + dot(low, data_high))


def forward_kernel(fh_ref, fl_ref, init_ref, x_ref, o_ref):
    rows = x_ref.shape[0] // 6
    lanes = x_ref.shape[1]
    mine = lax.axis_index("tm")
    y0, y1, p0, p1, t0, t1 = (x_ref[rows_of(rows, i, 6), :] for i in range(6))
    g0, g1 = (y * y * y * (1.0 / 3.0) + coupling * p for y, p in ((y0, p0), (y1, p1)))
    h0, h1 = (y * y * p - y + t for y, p, t in ((y0, p0, t0), (y1, p1, t1)))
    row = lax.broadcasted_iota(jnp.int32, (rows, lanes), 0)
    before = jnp.where(row == 0, init_ref[pl.ds(mine, 1), :], pltpu.roll(y1, 1, 0))
    after = jnp.where(row == rows - 1, 0.0, pltpu.roll(p0, rows - 1, 0))
    a0 = g0 + step_rate * (y0 - before)
    a1 = g1 + step_rate * (y1 - y0)
    b0 = h0 + step_rate * (p0 - p1)
    b1 = h1 + step_rate * (p1 - after)
    data = jnp.concatenate(
        [
            jnp.concatenate([a0, b0, y0, p0], 1),
            jnp.concatenate([a1, b1, y1, p1], 1),
        ],
        0,
    )
    hat = product(fh_ref[...], fl_ref[...], data)
    for f in range(2):
        for r in range(2):
            for q in range(2):
                column = (q * 2 + f) * lanes
                o_ref[rows_of(rows, (f * 2 + r) * 2 * rows + q, 2), :] = hat[
                    r * rows : (r + 1) * rows, column : column + lanes
                ]


def faces_kernel(m0_ref, m1_ref, m2_ref, m3_ref, cx, cyp, cym, czp, czm, bare, both, mat):
    item = lax.axis_index("space")
    for piece, ref in enumerate((m0_ref, m1_ref, m2_ref, m3_ref)):
        mat[item ^ piece] = ref[...]
    slabs, _, width, count_y, lanes = mat.shape
    count = slabs * width
    row = lax.broadcasted_iota(jnp.int32, (count_y, lanes), 0)
    lane = lax.broadcasted_iota(jnp.int32, (count_y, lanes), 1)

    def cond(x):
        return mat[x // width, 0, x % width]

    for x in range(count):
        c = cond(x)
        half = 0.5 * c
        up = 0.5 * (c + cond(x + 1)) if x + 1 < count else half
        down = 0.5 * (c + cond(x - 1)) if x > 0 else half
        cx[x] = up
        yp = jnp.where(row == count_y - 1, 0.0, 0.5 * pltpu.roll(c, count_y - 1, 0)) + half
        ym = jnp.where(row == 0, 0.0, 0.5 * pltpu.roll(c, 1, 0)) + half
        zp = jnp.where(lane == lanes - 1, 0.0, 0.5 * pltpu.roll(c, lanes - 1, 1)) + half
        zm = jnp.where(lane == 0, 0.0, 0.5 * pltpu.roll(c, 1, 1)) + half
        total = (up + down) + (yp + ym) + (zp + zm)
        bare[x] = total
        both[x] = total + mat[x // width, 1, x % width]
        cyp[x] = jnp.where(row == count_y - 1, 0.0, yp)
        cym[x] = jnp.where(row == 0, 0.0, ym)
        czp[x] = jnp.where(lane == lanes - 1, 0.0, zp)
        czm[x] = jnp.where(lane == 0, 0.0, zm)


def solve_kernel(co_ref, cx, cyp, cym, czp, czm, bare, both, x_ref, o_ref, diag, yy, res, d, t, w):
    slot = lax.axis_index("tm")
    item = lax.axis_index("space")
    cells = x_ref.shape[0] // 8
    slots = cells
    frequency = jnp.where((slot == 0) & (item % 2 == 1), slots, slot)
    base = frequency * COEF
    shift = co_ref[base]
    spread = co_ref[base + 1]
    start = co_ref[base + 2]
    slabs = 4
    count, count_y, lanes = d.shape
    width = count // slabs
    for s in range(slabs):
        res[s * width : (s + 1) * width] = x_ref[rows_of(cells, 2 * s * cells, 2), :].reshape(width, count_y, lanes)
        yy[s * width : (s + 1) * width] = x_ref[rows_of(cells, 2 * s * cells + 1, 2), :].reshape(width, count_y, lanes)

    def applied(ref, x, centre):
        v = ref[x]
        out = centre * v
        if x + 1 < count:
            out = out - cx[x] * ref[x + 1]
        if x > 0:
            out = out - cx[x - 1] * ref[x - 1]
        out = out - cyp[x] * pltpu.roll(v, count_y - 1, 0)
        out = out - cym[x] * pltpu.roll(v, 1, 0)
        out = out - czp[x] * pltpu.roll(v, lanes - 1, 1)
        out = out - czm[x] * pltpu.roll(v, 1, 1)
        return out

    for x in range(count):
        diag[x] = both[x] + shift
        r = res[x] + applied(yy, x, bare[x])
        first = start * r
        res[x] = r
        d[x] = first
        w[x] = first

    def step(i, carry):
        alpha = co_ref[base + 4 + 2 * i]
        beta = co_ref[base + 5 + 2 * i]
        for x in range(count):
            t[x] = applied(d, x, diag[x])
        for x in range(count):
            now = d[x]
            r = res[x] - (applied(t, x, diag[x]) + spread * now)
            now = alpha * now + beta * r
            res[x] = r
            d[x] = now
            w[x] = w[x] + now
        return carry

    lax.fori_loop(0, CHEB - 1, step, 0)
    for x in range(count):
        t[x] = applied(w, x, diag[x])
    for s in range(slabs):
        o_ref[rows_of(cells, 2 * s * cells, 2), :] = w[s * width : (s + 1) * width].reshape(width * count_y, lanes)
        o_ref[rows_of(cells, 2 * s * cells + 1, 2), :] = t[s * width : (s + 1) * width].reshape(width * count_y, lanes)


def inverse_kernel(gh_ref, gl_ref, b_ref, x_ref, o_ref):
    rows = x_ref.shape[0] // 8
    lanes = x_ref.shape[1]
    b = jnp.broadcast_to(b_ref[:, 0:1], (rows, lanes))
    u_re, ku_re, u_im, ku_im, v_re, kv_re, v_im, kv_im = (
        x_ref[rows_of(rows, i // 2 * 2 * rows + i % 2, 2), :] for i in range(8)
    )
    c00 = ku_re - (coupling * v_re - b * u_im)
    c01 = ku_im - (coupling * v_im + b * u_re)
    c10 = kv_re - (b * v_im - u_re)
    c11 = kv_im + (b * v_re + u_im)
    data = jnp.concatenate(
        [jnp.concatenate([c00, c10], 1), jnp.concatenate([c01, c11], 1)],
        0,
    )
    back = product(gh_ref[...], gl_ref[...], data)
    for f in range(2):
        for j in range(2):
            o_ref[rows_of(rows, f * 2 + j, 4), :] = back[
                j * rows : (j + 1) * rows, f * lanes : (f + 1) * lanes
            ]


def update_kernel(y_ref, p_ref, d_ref, ny_ref, np_ref):
    rows = y_ref.shape[1]
    for j in range(2):
        ny_ref[j] = y_ref[j] - d_ref[rows_of(rows, j, 4), :]
        np_ref[j] = p_ref[j] - d_ref[rows_of(rows, 2 + j, 4), :]


def swapped(value, distance):
    count = lax.axis_size("space")
    return lax.ppermute(value, "space", [(i, i ^ distance) for i in range(count)])


def shards(state_field, adjoint, target, initial_state, conductivity, reaction):
    steps, width_x, width_y, width_z = state_field.shape
    devices = lax.axis_size("tm")
    spaces = lax.axis_size("space")
    rows = width_x * width_y
    horizon = steps * devices
    assert steps == 2 and rows == devices and spaces == 4
    f32 = jnp.float32

    def shape(*dims):
        return jax.ShapeDtypeStruct(dims, f32)

    flat = (steps, rows, width_z)
    state_rows = state_field.reshape(flat)
    adjoint_rows = adjoint.reshape(flat)
    packed, material = pl.pallas_call(
        pack_kernel,
        out_shape=(
            shape(rows * 6, width_z),
            shape(2, width_x, width_y, width_z),
        ),
        in_specs=[hbm()] * 5,
        out_specs=(vmem(), vmem()),
        scratch_shapes=[pltpu.VMEM(flat, f32)] * 3 + [pltpu.SemaphoreType.DMA((5,))],
        name="pack",
    )(conductivity, reaction, state_rows, adjoint_rows, target.reshape(flat))
    table, twist = solver_table(horizon, devices)
    material_far = swapped(material, 2)
    material_core = swapped(material, 1)
    by_cell = lax.all_to_all(
        packed.reshape(rows * 3, 2, width_z), "tm", 0, 0, tiled=True
    ).reshape(packed.shape)
    by_cell, material_far = lax.optimization_barrier((by_cell, material_far))
    material_both = swapped(material_far, 1)
    forward, inverse = (halves(jnp.asarray(each)) for each in time_tables(horizon, devices))
    hat = pl.pallas_call(
        forward_kernel,
        out_shape=shape(devices * 8, width_z),
        in_specs=[vmem()] * 4,
        out_specs=vmem(),
        compiler_params=grant,
        name="forward",
    )(*forward, initial_state.reshape(rows, width_z), by_cell)
    everyone = ("space", "tm")
    by_item = lax.all_to_all(hat, everyone, 0, 0, tiled=True)
    grid = (spaces * width_x, width_y, width_z)
    faces = pl.pallas_call(
        faces_kernel,
        out_shape=(shape(*grid),) * 7,
        in_specs=[vmem()] * 4,
        out_specs=(vmem(),) * 7,
        scratch_shapes=[pltpu.VMEM((spaces, 2, width_x, width_y, width_z), f32)],
        compiler_params=grant,
        name="faces",
    )(material, material_core, material_far, material_both)
    solved = pl.pallas_call(
        solve_kernel,
        out_shape=shape(rows * 8, width_z),
        in_specs=[smem()] + [vmem()] * 8,
        out_specs=vmem(),
        scratch_shapes=[pltpu.VMEM(grid, f32)] * 6,
        compiler_params=grant,
        name="solve",
    )(jnp.asarray(table), *faces, by_item)
    by_row = lax.all_to_all(solved, everyone, 0, 0, tiled=True)
    delta = pl.pallas_call(
        inverse_kernel,
        out_shape=shape(devices * 4, width_z),
        in_specs=[vmem()] * 4,
        out_specs=vmem(),
        compiler_params=grant,
        name="inverse",
    )(*inverse, jnp.asarray(twist_block(twist)), by_row)
    by_time = lax.all_to_all(delta, "tm", 0, 0, tiled=True)
    new_state, new_adjoint = pl.pallas_call(
        update_kernel,
        out_shape=(shape(*flat), shape(*flat)),
        in_specs=[vmem()] * 3,
        out_specs=(vmem(), vmem()),
        compiler_params=grant,
        name="update",
    )(state_rows, adjoint_rows, by_time)
    return new_state.reshape(state_field.shape), new_adjoint.reshape(adjoint.shape)


def solution(mesh):
    in_specs = (
        P("tm", "space", None, None),
        P("tm", "space", None, None),
        P("tm", "space", None, None),
        P("space", None, None),
        P("space", None, None),
        P("space", None, None),
    )
    out_specs = (P("tm", "space", None, None), P("tm", "space", None, None))
    return jax.shard_map(shards, mesh=mesh, in_specs=in_specs, out_specs=out_specs, check_vma=False)
```

```python
import functools

import jax
import jax.numpy as jnp
import numpy as np
from jax import lax
from jax.experimental import pallas as pl
from jax.experimental.pallas import tpu as pltpu
from jax.sharding import PartitionSpec as P

CHEB = 8
step_rate = 2.0
coupling = 1.0
lower_edge = 0.05
upper_edge = 7.0
COEF = 32
vmem = functools.partial(pl.BlockSpec, memory_space=pltpu.VMEM)
grant = pltpu.CompilerParams(vmem_limit_bytes=8 * 1024 * 1024)
hbm = functools.partial(pl.BlockSpec, memory_space=pltpu.HBM)
smem = functools.partial(pl.BlockSpec, memory_space=pltpu.SMEM)


def time_tables(horizon, slots):
    k = np.arange(slots)[:, None]
    n = np.concatenate([np.arange(0, horizon, 2), np.arange(1, horizon, 2)])[None, :]
    angle = 2.0 * np.pi / horizon * ((k * n) % horizon)
    cosine, sine = np.cos(angle), np.sin(angle)
    alternation = np.where(n % 2 == 0, 1.0, -1.0)
    forward = np.concatenate([cosine, np.where(k == 0, alternation, -sine)], 0)
    inverse = (
        np.concatenate(
            [
                np.where(k == 0, 1.0, 2.0) * cosine,
                np.where(k == 0, alternation, -2.0 * sine),
            ],
            0,
        )
        / horizon
    )
    return forward.astype(np.float32), inverse.T.astype(np.float32)


def solver_table(horizon, slots):
    theta = 2.0 * np.pi / horizon * np.arange(slots + 1)
    shift = step_rate * (1.0 - np.cos(theta))
    twist = step_rate * np.sin(theta)
    twist[slots] = 0.0
    spread = twist * twist + coupling
    lower = (lower_edge + shift) ** 2 + spread
    upper = (upper_edge + shift) ** 2 + spread
    centre = 0.5 * (upper + lower)
    half = 0.5 * (upper - lower)
    ratio = centre / half
    rho = 1.0 / ratio
    table = np.zeros((slots + 1, COEF))
    table[:, 0] = shift
    table[:, 1] = spread
    table[:, 2] = 1.0 / centre
    for step in range(CHEB - 1):
        rho_next = 1.0 / (2.0 * ratio - rho)
        table[:, 4 + 2 * step] = rho_next * rho
        table[:, 5 + 2 * step] = 2.0 * rho_next / half
        rho = rho_next
    return table.reshape(-1).astype(np.float32), twist[:slots]


def twist_block(twist):
    block = np.zeros((twist.shape[0], 128), np.float32)
    block[:, 0] = twist
    return block


def rows_of(count, start, stride):
    return pl.ds(start, count, stride=stride)


def pack_kernel(c_hbm, r_hbm, y_hbm, p_hbm, t_hbm, o_ref, m_ref, y_ref, p_ref, t_ref, sem):
    copies = [
        pltpu.make_async_copy(source, target, sem.at[i])
        for i, (source, target) in enumerate(
            (
                (y_hbm, y_ref),
                (p_hbm, p_ref),
                (t_hbm, t_ref),
                (c_hbm, m_ref.at[0]),
                (r_hbm, m_ref.at[1]),
            )
        )
    ]
    for copy in copies:
        copy.start()
    for copy in copies:
        copy.wait()
    rows = y_ref.shape[1]
    for i, ref in enumerate((y_ref, p_ref, t_ref)):
        for j in range(2):
            o_ref[rows_of(rows, 2 * i + j, 6), :] = ref[j]


def halves(value):
    high = value.astype(jnp.bfloat16)
    return high, (value - high.astype(jnp.float32)).astype(jnp.bfloat16)


def product(high, low, data):
    data_high, data_low = halves(data)
    dot = functools.partial(lax.dot, preferred_element_type=jnp.float32)
    return dot(high, data_high) + (dot(high, data_low) + dot(low, data_high))


def forward_kernel(fh_ref, fl_ref, init_ref, x_ref, o_ref):
    rows = x_ref.shape[0] // 6
    lanes = x_ref.shape[1]
    mine = lax.axis_index("tm")
    y0, y1, p0, p1, t0, t1 = (x_ref[rows_of(rows, i, 6), :] for i in range(6))
    g0, g1 = (y * y * y * (1.0 / 3.0) + coupling * p for y, p in ((y0, p0), (y1, p1)))
    h0, h1 = (y * y * p - y + t for y, p, t in ((y0, p0, t0), (y1, p1, t1)))
    row = lax.broadcasted_iota(jnp.int32, (rows, lanes), 0)
    before = jnp.where(row == 0, init_ref[pl.ds(mine, 1), :], pltpu.roll(y1, 1, 0))
    after = jnp.where(row == rows - 1, 0.0, pltpu.roll(p0, rows - 1, 0))
    a0 = g0 + step_rate * (y0 - before)
    a1 = g1 + step_rate * (y1 - y0)
    b0 = h0 + step_rate * (p0 - p1)
    b1 = h1 + step_rate * (p1 - after)
    data = jnp.concatenate(
        [
            jnp.concatenate([a0, b0, y0, p0], 1),
            jnp.concatenate([a1, b1, y1, p1], 1),
        ],
        0,
    )
    hat = product(fh_ref[...], fl_ref[...], data)
    for f in range(2):
        for r in range(2):
            for q in range(2):
                column = (q * 2 + f) * lanes
                o_ref[rows_of(rows, (f * 2 + r) * 2 * rows + q, 2), :] = hat[
                    r * rows : (r + 1) * rows, column : column + lanes
                ]


def faces_kernel(m0_ref, m1_ref, m2_ref, m3_ref, cx, cyp, cym, czp, czm, bare, both, mat):
    item = lax.axis_index("space")
    for piece, ref in enumerate((m0_ref, m1_ref, m2_ref, m3_ref)):
        mat[item ^ piece] = ref[...]
    slabs, _, width, count_y, lanes = mat.shape
    count = slabs * width
    row = lax.broadcasted_iota(jnp.int32, (count_y, lanes), 0)
    lane = lax.broadcasted_iota(jnp.int32, (count_y, lanes), 1)

    def cond(x):
        return mat[x // width, 0, x % width]

    for x in range(count):
        c = cond(x)
        half = 0.5 * c
        up = 0.5 * (c + cond(x + 1)) if x + 1 < count else half
        down = 0.5 * (c + cond(x - 1)) if x > 0 else half
        cx[x] = up
        yp = jnp.where(row == count_y - 1, 0.0, 0.5 * pltpu.roll(c, count_y - 1, 0)) + half
        ym = jnp.where(row == 0, 0.0, 0.5 * pltpu.roll(c, 1, 0)) + half
        zp = jnp.where(lane == lanes - 1, 0.0, 0.5 * pltpu.roll(c, lanes - 1, 1)) + half
        zm = jnp.where(lane == 0, 0.0, 0.5 * pltpu.roll(c, 1, 1)) + half
        total = (up + down) + (yp + ym) + (zp + zm)
        bare[x] = total
        both[x] = total + mat[x // width, 1, x % width]
        cyp[x] = jnp.where(row == count_y - 1, 0.0, yp)
        cym[x] = jnp.where(row == 0, 0.0, ym)
        czp[x] = jnp.where(lane == lanes - 1, 0.0, zp)
        czm[x] = jnp.where(lane == 0, 0.0, zm)


def solve_kernel(co_ref, cx, cyp, cym, czp, czm, bare, both, x_ref, o_ref, diag, yy, res, d, t, w):
    slot = lax.axis_index("tm")
    item = lax.axis_index("space")
    cells = x_ref.shape[0] // 8
    slots = cells
    frequency = jnp.where((slot == 0) & (item % 2 == 1), slots, slot)
    base = frequency * COEF
    shift = co_ref[base]
    spread = co_ref[base + 1]
    start = co_ref[base + 2]
    slabs = 4
    count, count_y, lanes = d.shape
    width = count // slabs
    for s in range(slabs):
        res[s * width : (s + 1) * width] = x_ref[rows_of(cells, 2 * s * cells, 2), :].reshape(width, count_y, lanes)
        yy[s * width : (s + 1) * width] = x_ref[rows_of(cells, 2 * s * cells + 1, 2), :].reshape(width, count_y, lanes)

    def applied(ref, x, centre):
        v = ref[x]
        out = centre * v
        if x + 1 < count:
            out = out - cx[x] * ref[x + 1]
        if x > 0:
            out = out - cx[x - 1] * ref[x - 1]
        out = out - cyp[x] * pltpu.roll(v, count_y - 1, 0)
        out = out - cym[x] * pltpu.roll(v, 1, 0)
        out = out - czp[x] * pltpu.roll(v, lanes - 1, 1)
        out = out - czm[x] * pltpu.roll(v, 1, 1)
        return out

    for x in range(count):
        diag[x] = both[x] + shift
        r = res[x] + applied(yy, x, bare[x])
        first = start * r
        res[x] = r
        d[x] = first
        w[x] = first

    def step(i, carry):
        alpha = co_ref[base + 4 + 2 * i]
        beta = co_ref[base + 5 + 2 * i]
        for x in range(count):
            t[x] = applied(d, x, diag[x])
        for x in range(count):
            now = d[x]
            r = res[x] - (applied(t, x, diag[x]) + spread * now)
            now = alpha * now + beta * r
            res[x] = r
            d[x] = now
            w[x] = w[x] + now
        return carry

    lax.fori_loop(0, CHEB - 1, step, 0)
    for x in range(count):
        t[x] = applied(w, x, diag[x])
    for s in range(slabs):
        o_ref[rows_of(cells, 2 * s * cells, 2), :] = w[s * width : (s + 1) * width].reshape(width * count_y, lanes)
        o_ref[rows_of(cells, 2 * s * cells + 1, 2), :] = t[s * width : (s + 1) * width].reshape(width * count_y, lanes)


def inverse_kernel(gh_ref, gl_ref, b_ref, x_ref, o_ref):
    rows = x_ref.shape[0] // 8
    lanes = x_ref.shape[1]
    b = jnp.broadcast_to(b_ref[:, 0:1], (rows, lanes))
    u_re, ku_re, u_im, ku_im, v_re, kv_re, v_im, kv_im = (
        x_ref[rows_of(rows, i // 2 * 2 * rows + i % 2, 2), :] for i in range(8)
    )
    c00 = ku_re - (coupling * v_re - b * u_im)
    c01 = ku_im - (coupling * v_im + b * u_re)
    c10 = kv_re - (b * v_im - u_re)
    c11 = kv_im + (b * v_re + u_im)
    data = jnp.concatenate(
        [jnp.concatenate([c00, c10], 1), jnp.concatenate([c01, c11], 1)],
        0,
    )
    back = product(gh_ref[...], gl_ref[...], data)
    for f in range(2):
        for j in range(2):
            o_ref[rows_of(rows, f * 2 + j, 4), :] = back[
                j * rows : (j + 1) * rows, f * lanes : (f + 1) * lanes
            ]


def update_kernel(y_ref, p_ref, d_ref, ny_ref, np_ref):
    rows = y_ref.shape[1]
    for j in range(2):
        ny_ref[j] = y_ref[j] - d_ref[rows_of(rows, j, 4), :]
        np_ref[j] = p_ref[j] - d_ref[rows_of(rows, 2 + j, 4), :]


def swapped(value, distance):
    count = lax.axis_size("space")
    return lax.ppermute(value, "space", [(i, i ^ distance) for i in range(count)])


def shards(state_field, adjoint, target, initial_state, conductivity, reaction):
    steps, width_x, width_y, width_z = state_field.shape
    devices = lax.axis_size("tm")
    spaces = lax.axis_size("space")
    rows = width_x * width_y
    horizon = steps * devices
    assert steps == 2 and rows == devices and spaces == 4
    f32 = jnp.float32

    def shape(*dims):
        return jax.ShapeDtypeStruct(dims, f32)

    flat = (steps, rows, width_z)
    state_rows = state_field.reshape(flat)
    adjoint_rows = adjoint.reshape(flat)
    packed, material = pl.pallas_call(
        pack_kernel,
        out_shape=(
            shape(rows * 6, width_z),
            shape(2, width_x, width_y, width_z),
        ),
        in_specs=[hbm()] * 5,
        out_specs=(vmem(), vmem()),
        scratch_shapes=[pltpu.VMEM(flat, f32)] * 3 + [pltpu.SemaphoreType.DMA((5,))],
        name="pack",
    )(conductivity, reaction, state_rows, adjoint_rows, target.reshape(flat))
    table, twist = solver_table(horizon, devices)
    material_far = swapped(material, 2)
    material_core = swapped(material, 1)
    by_cell = lax.all_to_all(
        packed.reshape(rows * 3, 2, width_z), "tm", 0, 0, tiled=True
    ).reshape(packed.shape)
    by_cell, material_far = lax.optimization_barrier((by_cell, material_far))
    material_both = swapped(material_far, 1)
    forward, inverse = (halves(jnp.asarray(each)) for each in time_tables(horizon, devices))
    hat = pl.pallas_call(
        forward_kernel,
        out_shape=shape(devices * 8, width_z),
        in_specs=[vmem()] * 4,
        out_specs=vmem(),
        compiler_params=grant,
        name="forward",
    )(*forward, initial_state.reshape(rows, width_z), by_cell)
    grid = (spaces * width_x, width_y, width_z)
    faces = pl.pallas_call(
        faces_kernel,
        out_shape=(shape(*grid),) * 7,
        in_specs=[vmem()] * 4,
        out_specs=(vmem(),) * 7,
        scratch_shapes=[pltpu.VMEM((spaces, 2, width_x, width_y, width_z), f32)],
        compiler_params=grant,
        name="faces",
    )(material, material_core, material_far, material_both)
    hat, faces = lax.optimization_barrier((hat, faces))
    everyone = ("space", "tm")
    by_item = lax.all_to_all(hat, everyone, 0, 0, tiled=True)
    solved = pl.pallas_call(
        solve_kernel,
        out_shape=shape(rows * 8, width_z),
        in_specs=[smem()] + [vmem()] * 8,
        out_specs=vmem(),
        scratch_shapes=[pltpu.VMEM(grid, f32)] * 6,
        compiler_params=grant,
        name="solve",
    )(jnp.asarray(table), *faces, by_item)
    by_row = lax.all_to_all(solved, everyone, 0, 0, tiled=True)
    delta = pl.pallas_call(
        inverse_kernel,
        out_shape=shape(devices * 4, width_z),
        in_specs=[vmem()] * 4,
        out_specs=vmem(),
        compiler_params=grant,
        name="inverse",
    )(*inverse, jnp.asarray(twist_block(twist)), by_row)
    by_time = lax.all_to_all(delta, "tm", 0, 0, tiled=True)
    new_state, new_adjoint = pl.pallas_call(
        update_kernel,
        out_shape=(shape(*flat), shape(*flat)),
        in_specs=[vmem()] * 3,
        out_specs=(vmem(), vmem()),
        compiler_params=grant,
        name="update",
    )(state_rows, adjoint_rows, by_time)
    return new_state.reshape(state_field.shape), new_adjoint.reshape(adjoint.shape)


def solution(mesh):
    in_specs = (
        P("tm", "space", None, None),
        P("tm", "space", None, None),
        P("tm", "space", None, None),
        P("space", None, None),
        P("space", None, None),
        P("space", None, None),
    )
    out_specs = (P("tm", "space", None, None), P("tm", "space", None, None))
    return jax.shard_map(shards, mesh=mesh, in_specs=in_specs, out_specs=out_specs, check_vma=False)
```

```python
import functools

import jax
import jax.numpy as jnp
import numpy as np
from jax import lax
from jax.experimental import pallas as pl
from jax.experimental.pallas import tpu as pltpu
from jax.sharding import PartitionSpec as P

CHEB = 8
step_rate = 2.0
coupling = 1.0
lower_edge = 0.05
upper_edge = 7.0
COEF = 32
vmem = functools.partial(pl.BlockSpec, memory_space=pltpu.VMEM)
grant = pltpu.CompilerParams(vmem_limit_bytes=8 * 1024 * 1024)
hbm = functools.partial(pl.BlockSpec, memory_space=pltpu.HBM)
smem = functools.partial(pl.BlockSpec, memory_space=pltpu.SMEM)


def time_tables(horizon, slots):
    k = np.arange(slots)[:, None]
    n = np.concatenate([np.arange(0, horizon, 2), np.arange(1, horizon, 2)])[None, :]
    angle = 2.0 * np.pi / horizon * ((k * n) % horizon)
    cosine, sine = np.cos(angle), np.sin(angle)
    alternation = np.where(n % 2 == 0, 1.0, -1.0)
    forward = np.concatenate([cosine, np.where(k == 0, alternation, -sine)], 0)
    inverse = (
        np.concatenate(
            [
                np.where(k == 0, 1.0, 2.0) * cosine,
                np.where(k == 0, alternation, -2.0 * sine),
            ],
            0,
        )
        / horizon
    )
    return forward.astype(np.float32), inverse.T.astype(np.float32)


def solver_table(horizon, slots):
    theta = 2.0 * np.pi / horizon * np.arange(slots + 1)
    shift = step_rate * (1.0 - np.cos(theta))
    twist = step_rate * np.sin(theta)
    twist[slots] = 0.0
    spread = twist * twist + coupling
    lower = (lower_edge + shift) ** 2 + spread
    upper = (upper_edge + shift) ** 2 + spread
    centre = 0.5 * (upper + lower)
    half = 0.5 * (upper - lower)
    ratio = centre / half
    gamma = np.sqrt(2.0 / half)
    offset = np.sqrt(2.0 * (centre - spread) / half)
    table = np.zeros((slots + 1, COEF))
    table[:, 0] = gamma
    table[:, 1] = offset
    table[:, 2] = shift
    table[:, 3] = 1.0 / gamma
    table[:, 4] = offset / gamma
    nodes = np.pi * (np.arange(CHEB) + 0.5) / CHEB
    points = np.cos(nodes)[None, :]
    value = centre[:, None] + half[:, None] * points
    top = np.cosh(CHEB * np.arccosh(ratio))[:, None]
    samples = (1.0 - np.cos(CHEB * np.arccos(-points)) / top) / value
    for j in range(CHEB):
        weight = (1.0 if j == 0 else 2.0) / CHEB
        table[:, 8 + j] = weight * np.sum(samples * np.cos(j * nodes)[None, :], 1)
    return table.reshape(-1).astype(np.float32), twist[:slots]


def twist_block(twist):
    block = np.zeros((twist.shape[0], 128), np.float32)
    block[:, 0] = twist
    return block


def rows_of(count, start, stride):
    return pl.ds(start, count, stride=stride)


def pack_kernel(c_hbm, r_hbm, y_hbm, p_hbm, t_hbm, o_ref, m_ref, y_ref, p_ref, t_ref, sem):
    copies = [
        pltpu.make_async_copy(source, target, sem.at[i])
        for i, (source, target) in enumerate(
            (
                (y_hbm, y_ref),
                (p_hbm, p_ref),
                (t_hbm, t_ref),
                (c_hbm, m_ref.at[0]),
                (r_hbm, m_ref.at[1]),
            )
        )
    ]
    for copy in copies:
        copy.start()
    for copy in copies:
        copy.wait()
    rows = y_ref.shape[1]
    for i, ref in enumerate((y_ref, p_ref, t_ref)):
        for j in range(2):
            o_ref[rows_of(rows, 2 * i + j, 6), :] = ref[j]


def halves(value):
    high = value.astype(jnp.bfloat16)
    return high, (value - high.astype(jnp.float32)).astype(jnp.bfloat16)


def product(high, low, data):
    data_high, data_low = halves(data)
    dot = functools.partial(lax.dot, preferred_element_type=jnp.float32)
    return dot(high, data_high) + (dot(high, data_low) + dot(low, data_high))


def forward_kernel(fh_ref, fl_ref, init_ref, x_ref, o_ref):
    rows = x_ref.shape[0] // 6
    lanes = x_ref.shape[1]
    mine = lax.axis_index("tm")
    y0, y1, p0, p1, t0, t1 = (x_ref[rows_of(rows, i, 6), :] for i in range(6))
    g0, g1 = (y * y * y * (1.0 / 3.0) + coupling * p for y, p in ((y0, p0), (y1, p1)))
    h0, h1 = (y * y * p - y + t for y, p, t in ((y0, p0, t0), (y1, p1, t1)))
    row = lax.broadcasted_iota(jnp.int32, (rows, lanes), 0)
    before = jnp.where(row == 0, init_ref[pl.ds(mine, 1), :], pltpu.roll(y1, 1, 0))
    after = jnp.where(row == rows - 1, 0.0, pltpu.roll(p0, rows - 1, 0))
    a0 = g0 + step_rate * (y0 - before)
    a1 = g1 + step_rate * (y1 - y0)
    b0 = h0 + step_rate * (p0 - p1)
    b1 = h1 + step_rate * (p1 - after)
    data = jnp.concatenate(
        [
            jnp.concatenate([a0, b0, y0, p0], 1),
            jnp.concatenate([a1, b1, y1, p1], 1),
        ],
        0,
    )
    hat = product(fh_ref[...], fl_ref[...], data)
    for f in range(2):
        for r in range(2):
            for q in range(2):
                column = (q * 2 + f) * lanes
                o_ref[rows_of(rows, (f * 2 + r) * 2 * rows + q, 2), :] = hat[
                    r * rows : (r + 1) * rows, column : column + lanes
                ]


def coefficients(slots):
    slot = lax.axis_index("tm")
    item = lax.axis_index("space")
    return item, jnp.where((slot == 0) & (item % 2 == 1), slots, slot) * COEF


def faces_kernel(
    slots,
    co_ref,
    m0_ref,
    m1_ref,
    m2_ref,
    m3_ref,
    cx,
    cy,
    cy_next,
    cy_last,
    cz_next,
    cz_last,
    bare,
    plus,
    minus,
    mat,
):
    item, base = coefficients(slots)
    gamma = co_ref[base]
    offset = co_ref[base + 1]
    shift = co_ref[base + 2]
    for piece, ref in enumerate((m0_ref, m1_ref, m2_ref, m3_ref)):
        mat[item ^ piece] = ref[...]
    count, _, subs, lanes = cx.shape
    width = mat.shape[2]
    sub = lax.broadcasted_iota(jnp.int32, (subs, lanes), 0)
    lane = lax.broadcasted_iota(jnp.int32, (subs, lanes), 1)
    first, last = sub == 0, sub == subs - 1
    left, right = lane == 0, lane == lanes - 1

    def part(which, x, parity):
        return mat.at[x // width, which, x % width][rows_of(subs, parity, 2), :]

    for x in range(count):
        even, odd = part(0, x, 0), part(0, x, 1)
        pair = 0.5 * (even + odd)
        after = 0.5 * odd + jnp.where(last, 0.0, 0.5 * pltpu.roll(even, subs - 1, 0))
        before = 0.5 * even + jnp.where(first, 0.0, 0.5 * pltpu.roll(odd, 1, 0))
        cy[x] = gamma * pair
        cy_next[x] = gamma * jnp.where(last, 0.0, after)
        cy_last[x] = gamma * jnp.where(first, 0.0, before)
        for parity, (c, side) in enumerate(((even, before), (odd, after))):
            half = 0.5 * c
            up = half + 0.5 * part(0, x + 1, parity) if x + 1 < count else half
            down = half + 0.5 * part(0, x - 1, parity) if x > 0 else half
            zn = half + jnp.where(right, 0.0, 0.5 * pltpu.roll(c, lanes - 1, 1))
            zl = half + jnp.where(left, 0.0, 0.5 * pltpu.roll(c, 1, 1))
            cx[x, parity] = gamma * up
            cz_next[x, parity] = gamma * jnp.where(right, 0.0, zn)
            cz_last[x, parity] = gamma * jnp.where(left, 0.0, zl)
            total = (up + down) + (pair + side) + (zn + zl)
            bare[x, parity] = gamma * total
            full = gamma * (total + part(1, x, parity) + shift)
            plus[x, parity] = full + offset
            minus[x, parity] = full - offset


def solve_kernel(
    slots,
    co_ref,
    cx,
    cy,
    cy_next,
    cy_last,
    cz_next,
    cz_last,
    bare,
    plus,
    minus,
    x_ref,
    o_ref,
    res,
    b0,
    b1,
    t,
):
    base = coefficients(slots)[1]
    count, _, subs, lanes = cx.shape
    cells = x_ref.shape[0] // 8
    line = 2 * subs
    width = cells // line

    def place(x, parity, field):
        start = (x // width * cells + x % width * line + parity) * 2 + field
        return rows_of(subs, start, 4)

    def sweep(load, diag, emit):
        now, cx_now = load(0), None
        last = cx_last = None
        for x in range(count):
            after = load(x + 1) if x + 1 < count else None
            cx_now = (cx[x, 0], cx[x, 1]) if x + 1 < count else None
            pair = cy[x]
            side = (
                pair * now[1] + cy_last[x] * pltpu.roll(now[1], 1, 0),
                pair * now[0] + cy_next[x] * pltpu.roll(now[0], subs - 1, 0),
            )
            for parity in range(2):
                v = now[parity]
                out = diag[x, parity] * v - side[parity]
                lateral = cz_next[x, parity] * pltpu.roll(v, lanes - 1, 1)
                lateral = lateral + cz_last[x, parity] * pltpu.roll(v, 1, 1)
                if after is not None:
                    out = out - cx_now[parity] * after[parity]
                if last is not None:
                    lateral = lateral + cx_last[parity] * last[parity]
                emit(x, parity, out - lateral, v)
            last, now, cx_last = now, after, cx_now

    def kept(ref):
        return lambda x: (ref[x, 0], ref[x, 1])

    inverse_gamma = co_ref[base + 3]
    top = co_ref[base + 8 + CHEB - 1]

    def begin(x, parity, out, v):
        r = x_ref[place(x, parity, 0), :] + inverse_gamma * out
        res[x, parity] = r
        b0[x, parity] = top * r
        b1[x, parity] = jnp.zeros_like(r)

    sweep(
        lambda x: (x_ref[place(x, 0, 1), :], x_ref[place(x, 1, 1), :]),
        bare,
        begin,
    )

    def first_factor(source):
        def keep(x, parity, out, v):
            t[x, parity] = out

        sweep(kept(source), plus, keep)

    def clenshaw(source, target, weight):
        def keep(x, parity, out, v):
            target[x, parity] = (weight * res[x, parity] - target[x, parity]) + out

        first_factor(source)
        sweep(kept(t), minus, keep)

    def two_steps(i, carry):
        at = base + 8 + CHEB - 2 - 2 * i
        clenshaw(b0, b1, co_ref[at])
        clenshaw(b1, b0, co_ref[at - 1])
        return carry

    lax.fori_loop(0, (CHEB - 2) // 2, two_steps, 0)
    weight = co_ref[base + 8]
    offset = co_ref[base + 4]

    def finish(x, parity, out, v):
        w = (weight * res[x, parity] - b1[x, parity]) + 0.5 * out
        b1[x, parity] = w
        o_ref[place(x, parity, 0), :] = w

    first_factor(b0)
    sweep(kept(t), minus, finish)

    def image(x, parity, out, v):
        o_ref[place(x, parity, 1), :] = inverse_gamma * out - offset * v

    sweep(kept(b1), plus, image)


def inverse_kernel(gh_ref, gl_ref, b_ref, x_ref, o_ref):
    rows = x_ref.shape[0] // 8
    lanes = x_ref.shape[1]
    b = jnp.broadcast_to(b_ref[:, 0:1], (rows, lanes))
    u_re, ku_re, u_im, ku_im, v_re, kv_re, v_im, kv_im = (
        x_ref[rows_of(rows, i // 2 * 2 * rows + i % 2, 2), :] for i in range(8)
    )
    c00 = ku_re - (coupling * v_re - b * u_im)
    c01 = ku_im - (coupling * v_im + b * u_re)
    c10 = kv_re - (b * v_im - u_re)
    c11 = kv_im + (b * v_re + u_im)
    data = jnp.concatenate(
        [jnp.concatenate([c00, c10], 1), jnp.concatenate([c01, c11], 1)],
        0,
    )
    back = product(gh_ref[...], gl_ref[...], data)
    for f in range(2):
        for j in range(2):
            o_ref[rows_of(rows, f * 2 + j, 4), :] = back[
                j * rows : (j + 1) * rows, f * lanes : (f + 1) * lanes
            ]


def update_kernel(y_ref, p_ref, d_ref, ny_ref, np_ref):
    rows = y_ref.shape[1]
    for j in range(2):
        ny_ref[j] = y_ref[j] - d_ref[rows_of(rows, j, 4), :]
        np_ref[j] = p_ref[j] - d_ref[rows_of(rows, 2 + j, 4), :]


def swapped(value, distance):
    count = lax.axis_size("space")
    return lax.ppermute(value, "space", [(i, i ^ distance) for i in range(count)])


def shards(state_field, adjoint, target, initial_state, conductivity, reaction):
    steps, width_x, width_y, width_z = state_field.shape
    devices = lax.axis_size("tm")
    spaces = lax.axis_size("space")
    rows = width_x * width_y
    horizon = steps * devices
    assert steps == 2 and rows == devices and spaces == 4
    f32 = jnp.float32

    def shape(*dims):
        return jax.ShapeDtypeStruct(dims, f32)

    flat = (steps, rows, width_z)
    state_rows = state_field.reshape(flat)
    adjoint_rows = adjoint.reshape(flat)
    packed, material = pl.pallas_call(
        pack_kernel,
        out_shape=(
            shape(rows * 6, width_z),
            shape(2, width_x, width_y, width_z),
        ),
        in_specs=[hbm()] * 5,
        out_specs=(vmem(), vmem()),
        scratch_shapes=[pltpu.VMEM(flat, f32)] * 3 + [pltpu.SemaphoreType.DMA((5,))],
        name="pack",
    )(conductivity, reaction, state_rows, adjoint_rows, target.reshape(flat))
    table, twist = solver_table(horizon, devices)
    material_far = swapped(material, 2)
    material_core = swapped(material, 1)
    by_cell = lax.all_to_all(
        packed.reshape(rows * 3, 2, width_z), "tm", 0, 0, tiled=True
    ).reshape(packed.shape)
    by_cell, material_far = lax.optimization_barrier((by_cell, material_far))
    material_both = swapped(material_far, 1)
    forward, inverse = (halves(jnp.asarray(each)) for each in time_tables(horizon, devices))
    hat = pl.pallas_call(
        forward_kernel,
        out_shape=shape(devices * 8, width_z),
        in_specs=[vmem()] * 4,
        out_specs=vmem(),
        compiler_params=grant,
        name="forward",
    )(*forward, initial_state.reshape(rows, width_z), by_cell)
    grid = (spaces * width_x, 2, width_y // 2, width_z)
    pairs = (spaces * width_x, width_y // 2, width_z)
    faces = pl.pallas_call(
        functools.partial(faces_kernel, devices),
        out_shape=(shape(*grid),) + (shape(*pairs),) * 3 + (shape(*grid),) * 5,
        in_specs=[smem()] + [vmem()] * 4,
        out_specs=(vmem(),) * 9,
        scratch_shapes=[pltpu.VMEM((spaces, 2, width_x, width_y, width_z), f32)],
        compiler_params=grant,
        name="faces",
    )(jnp.asarray(table), material, material_core, material_far, material_both)
    hat, faces = lax.optimization_barrier((hat, faces))
    everyone = ("space", "tm")
    by_item = lax.all_to_all(hat, everyone, 0, 0, tiled=True)
    solved = pl.pallas_call(
        functools.partial(solve_kernel, devices),
        out_shape=shape(rows * 8, width_z),
        in_specs=[smem()] + [vmem()] * 10,
        out_specs=vmem(),
        scratch_shapes=[pltpu.VMEM(grid, f32)] * 4,
        compiler_params=grant,
        name="solve",
    )(jnp.asarray(table), *faces, by_item)
    by_row = lax.all_to_all(solved, everyone, 0, 0, tiled=True)
    delta = pl.pallas_call(
        inverse_kernel,
        out_shape=shape(devices * 4, width_z),
        in_specs=[vmem()] * 4,
        out_specs=vmem(),
        compiler_params=grant,
        name="inverse",
    )(*inverse, jnp.asarray(twist_block(twist)), by_row)
    by_time = lax.all_to_all(delta, "tm", 0, 0, tiled=True)
    new_state, new_adjoint = pl.pallas_call(
        update_kernel,
        out_shape=(shape(*flat), shape(*flat)),
        in_specs=[vmem()] * 3,
        out_specs=(vmem(), vmem()),
        compiler_params=grant,
        name="update",
    )(state_rows, adjoint_rows, by_time)
    return new_state.reshape(state_field.shape), new_adjoint.reshape(adjoint.shape)


def solution(mesh):
    in_specs = (
        P("tm", "space", None, None),
        P("tm", "space", None, None),
        P("tm", "space", None, None),
        P("space", None, None),
        P("space", None, None),
        P("space", None, None),
    )
    out_specs = (P("tm", "space", None, None), P("tm", "space", None, None))
    return jax.shard_map(shards, mesh=mesh, in_specs=in_specs, out_specs=out_specs, check_vma=False)
```

```python
import functools

import jax
import jax.numpy as jnp
import numpy as np
from jax import lax
from jax.experimental import pallas as pl
from jax.experimental.pallas import tpu as pltpu
from jax.sharding import PartitionSpec as P


CHEB = 8
step_rate = 2.0
coupling = 1.0
lower_edge = 0.05
upper_edge = 7.0
COEF = 16
vmem = functools.partial(pl.BlockSpec, memory_space=pltpu.VMEM)
grant = pltpu.CompilerParams(vmem_limit_bytes=8 * 1024 * 1024)
hbm = functools.partial(pl.BlockSpec, memory_space=pltpu.HBM)


def time_tables(horizon, slots):
    k = np.arange(slots)[:, None]
    n = np.concatenate([np.arange(0, horizon, 2), np.arange(1, horizon, 2)])[None, :]
    angle = 2.0 * np.pi / horizon * ((k * n) % horizon)
    cosine, sine = np.cos(angle), np.sin(angle)
    alternation = np.where(n % 2 == 0, 1.0, -1.0)
    forward = np.concatenate([cosine, np.where(k == 0, alternation, -sine)], 0)
    inverse = (
        np.concatenate(
            [
                np.where(k == 0, 1.0, 2.0) * cosine,
                np.where(k == 0, alternation, -2.0 * sine),
            ],
            0,
        )
        / horizon
    )
    return forward.astype(np.float32), inverse.T.astype(np.float32)


def solver_table(horizon, slots):
    theta = 2.0 * np.pi / horizon * np.arange(slots + 1)
    shift = step_rate * (1.0 - np.cos(theta))
    twist = step_rate * np.sin(theta)
    twist[slots] = 0.0
    spread = twist * twist + coupling
    lower = (lower_edge + shift) ** 2 + spread
    upper = (upper_edge + shift) ** 2 + spread
    centre = 0.5 * (upper + lower)
    half = 0.5 * (upper - lower)
    ratio = centre / half
    gamma = np.sqrt(2.0 / half)
    offset = np.sqrt(2.0 * (centre - spread) / half)
    table = np.zeros((slots + 1, COEF))
    table[:, 0] = gamma
    table[:, 1] = offset
    table[:, 2] = shift
    table[:, 3] = 1.0 / gamma
    table[:, 4] = offset / gamma
    nodes = np.pi * (np.arange(CHEB) + 0.5) / CHEB
    points = np.cos(nodes)[None, :]
    value = centre[:, None] + half[:, None] * points
    top = np.cosh(CHEB * np.arccosh(ratio))[:, None]
    samples = (1.0 - np.cos(CHEB * np.arccos(-points)) / top) / value
    for j in range(CHEB):
        weight = (1.0 if j == 0 else 2.0) / CHEB
        table[:, 5 + j] = weight * np.sum(samples * np.cos(j * nodes)[None, :], 1)
    rows = np.broadcast_to(table.reshape(-1, 1), (table.size, 128))
    return rows.astype(np.float32), twist[:slots]


def twist_block(twist):
    block = np.zeros((twist.shape[0], 128), np.float32)
    block[:, 0] = twist
    return block


def rows_of(count, start, stride):
    return pl.ds(start, count, stride=stride)


def pack_kernel(c_hbm, r_hbm, y_hbm, p_hbm, t_hbm, o_ref, m_ref, y_ref, p_ref, t_ref, sem):
    copies = [
        pltpu.make_async_copy(source, target, sem.at[i])
        for i, (source, target) in enumerate(
            (
                (y_hbm, y_ref),
                (p_hbm, p_ref),
                (t_hbm, t_ref),
                (c_hbm, m_ref.at[0]),
                (r_hbm, m_ref.at[1]),
            )
        )
    ]
    for copy in copies:
        copy.start()
    for copy in copies:
        copy.wait()
    rows = y_ref.shape[1]
    for i, ref in enumerate((y_ref, p_ref, t_ref)):
        for j in range(2):
            o_ref[rows_of(rows, 2 * i + j, 6), :] = ref[j]


def halves(value):
    high = value.astype(jnp.bfloat16)
    return high, (value - high.astype(jnp.float32)).astype(jnp.bfloat16)


def product(high, low, data):
    data_high, data_low = halves(data)
    dot = functools.partial(lax.dot, preferred_element_type=jnp.float32)
    return dot(high, data_high) + (dot(high, data_low) + dot(low, data_high))


def forward_kernel(fh_ref, fl_ref, init_ref, x_ref, o_ref):
    rows = x_ref.shape[0] // 6
    lanes = x_ref.shape[1]
    mine = lax.axis_index("tm")
    y0, y1, p0, p1, t0, t1 = (x_ref[rows_of(rows, i, 6), :] for i in range(6))
    g0, g1 = (y * y * y * (1.0 / 3.0) + coupling * p for y, p in ((y0, p0), (y1, p1)))
    h0, h1 = (y * y * p - y + t for y, p, t in ((y0, p0, t0), (y1, p1, t1)))
    row = lax.broadcasted_iota(jnp.int32, (rows, lanes), 0)
    before = jnp.where(row == 0, init_ref[pl.ds(mine, 1), :], pltpu.roll(y1, 1, 0))
    after = jnp.where(row == rows - 1, 0.0, pltpu.roll(p0, rows - 1, 0))
    a0 = g0 + step_rate * (y0 - before)
    a1 = g1 + step_rate * (y1 - y0)
    b0 = h0 + step_rate * (p0 - p1)
    b1 = h1 + step_rate * (p1 - after)
    data = jnp.concatenate(
        [
            jnp.concatenate([a0, b0, y0, p0], 1),
            jnp.concatenate([a1, b1, y1, p1], 1),
        ],
        0,
    )
    hat = product(fh_ref[...], fl_ref[...], data)
    for f in range(2):
        for r in range(2):
            for q in range(2):
                column = (q * 2 + f) * lanes
                o_ref[rows_of(rows, (f * 2 + r) * 2 * rows + q, 2), :] = hat[
                    r * rows : (r + 1) * rows, column : column + lanes
                ]


def coefficients(co_ref, slots, subs):
    slot = lax.axis_index("tm")
    item = lax.axis_index("space")
    base = jnp.where((slot == 0) & (item % 2 == 1), slots, slot) * COEF
    lanes = co_ref.shape[1]
    return item, lambda j: jnp.broadcast_to(co_ref[pl.ds(base + j, 1), :], (subs, lanes))


def faces_kernel(
    slots,
    co_ref,
    m0_ref,
    m1_ref,
    m2_ref,
    m3_ref,
    cx,
    cy,
    cy_next,
    cy_last,
    cz_next,
    cz_last,
    bare,
    plus,
    minus,
    mat,
):
    item, coefficient = coefficients(co_ref, slots, cx.shape[2])
    gamma, offset, shift = (coefficient(j) for j in range(3))
    for piece, ref in enumerate((m0_ref, m1_ref, m2_ref, m3_ref)):
        mat[item ^ piece] = ref[...]
    count, _, subs, lanes = cx.shape
    width = mat.shape[2]
    sub = lax.broadcasted_iota(jnp.int32, (subs, lanes), 0)
    lane = lax.broadcasted_iota(jnp.int32, (subs, lanes), 1)
    first, last = sub == 0, sub == subs - 1
    left, right = lane == 0, lane == lanes - 1

    def part(which, x, parity):
        return mat.at[x // width, which, x % width][rows_of(subs, parity, 2), :]

    for x in range(count):
        even, odd = part(0, x, 0), part(0, x, 1)
        pair = 0.5 * (even + odd)
        after = 0.5 * odd + jnp.where(last, 0.0, 0.5 * pltpu.roll(even, subs - 1, 0))
        before = 0.5 * even + jnp.where(first, 0.0, 0.5 * pltpu.roll(odd, 1, 0))
        cy[x] = gamma * pair
        cy_next[x] = gamma * jnp.where(last, 0.0, after)
        cy_last[x] = gamma * jnp.where(first, 0.0, before)
        for parity, (c, side) in enumerate(((even, before), (odd, after))):
            half = 0.5 * c
            up = half + 0.5 * part(0, x + 1, parity) if x + 1 < count else half
            down = half + 0.5 * part(0, x - 1, parity) if x > 0 else half
            zn = half + jnp.where(right, 0.0, 0.5 * pltpu.roll(c, lanes - 1, 1))
            zl = half + jnp.where(left, 0.0, 0.5 * pltpu.roll(c, 1, 1))
            cx[x, parity] = gamma * up
            cz_next[x, parity] = gamma * jnp.where(right, 0.0, zn)
            cz_last[x, parity] = gamma * jnp.where(left, 0.0, zl)
            total = (up + down) + (pair + side) + (zn + zl)
            bare[x, parity] = gamma * total
            full = gamma * (total + part(1, x, parity) + shift)
            plus[x, parity] = full + offset
            minus[x, parity] = full - offset


def solve_kernel(
    slots,
    co_ref,
    cx,
    cy,
    cy_next,
    cy_last,
    cz_next,
    cz_last,
    bare,
    plus,
    minus,
    x_ref,
    o_ref,
    res,
    b0,
    b1,
    t,
):
    count, _, subs, lanes = cx.shape
    coefficient = coefficients(co_ref, slots, subs)[1]
    cells = x_ref.shape[0] // 8
    line = 2 * subs
    width = cells // line

    def place(x, parity, field):
        start = (x // width * cells + x % width * line + parity) * 2 + field
        return rows_of(subs, start, 4)

    def sweep(load, diag, emit):
        now, cx_now = load(0), None
        last = cx_last = None
        for x in range(count):
            after = load(x + 1) if x + 1 < count else None
            cx_now = (cx[x, 0], cx[x, 1]) if x + 1 < count else None
            pair = cy[x]
            side = (
                pair * now[1] + cy_last[x] * pltpu.roll(now[1], 1, 0),
                pair * now[0] + cy_next[x] * pltpu.roll(now[0], subs - 1, 0),
            )
            for parity in range(2):
                v = now[parity]
                out = diag[x, parity] * v - side[parity]
                lateral = cz_next[x, parity] * pltpu.roll(v, lanes - 1, 1)
                lateral = lateral + cz_last[x, parity] * pltpu.roll(v, 1, 1)
                if after is not None:
                    out = out - cx_now[parity] * after[parity]
                if last is not None:
                    lateral = lateral + cx_last[parity] * last[parity]
                emit(x, parity, out - lateral, v)
            last, now, cx_last = now, after, cx_now

    def kept(ref):
        return lambda x: (ref[x, 0], ref[x, 1])

    inverse_gamma = coefficient(3)
    top = coefficient(5 + CHEB - 1)

    def begin(x, parity, out, v):
        r = x_ref[place(x, parity, 0), :] + inverse_gamma * out
        res[x, parity] = r
        b0[x, parity] = top * r
        b1[x, parity] = jnp.zeros_like(r)

    sweep(
        lambda x: (x_ref[place(x, 0, 1), :], x_ref[place(x, 1, 1), :]),
        bare,
        begin,
    )

    def first_factor(source):
        def keep(x, parity, out, v):
            t[x, parity] = out

        sweep(kept(source), plus, keep)

    def clenshaw(source, target, weight):
        def keep(x, parity, out, v):
            target[x, parity] = (weight * res[x, parity] - target[x, parity]) + out

        first_factor(source)
        sweep(kept(t), minus, keep)

    def two_steps(i, carry):
        at = 5 + CHEB - 2 - 2 * i
        clenshaw(b0, b1, coefficient(at))
        clenshaw(b1, b0, coefficient(at - 1))
        return carry

    lax.fori_loop(0, (CHEB - 2) // 2, two_steps, 0)
    weight = coefficient(5)
    offset = coefficient(4)

    def finish(x, parity, out, v):
        w = (weight * res[x, parity] - b1[x, parity]) + 0.5 * out
        b1[x, parity] = w
        o_ref[place(x, parity, 0), :] = w

    first_factor(b0)
    sweep(kept(t), minus, finish)

    def image(x, parity, out, v):
        o_ref[place(x, parity, 1), :] = inverse_gamma * out - offset * v

    sweep(kept(b1), plus, image)


def inverse_kernel(gh_ref, gl_ref, b_ref, x_ref, o_ref):
    rows = x_ref.shape[0] // 8
    lanes = x_ref.shape[1]
    b = jnp.broadcast_to(b_ref[:, 0:1], (rows, lanes))
    u_re, ku_re, u_im, ku_im, v_re, kv_re, v_im, kv_im = (
        x_ref[rows_of(rows, i // 2 * 2 * rows + i % 2, 2), :] for i in range(8)
    )
    c00 = ku_re - (coupling * v_re - b * u_im)
    c01 = ku_im - (coupling * v_im + b * u_re)
    c10 = kv_re - (b * v_im - u_re)
    c11 = kv_im + (b * v_re + u_im)
    data = jnp.concatenate(
        [jnp.concatenate([c00, c10], 1), jnp.concatenate([c01, c11], 1)],
        0,
    )
    back = product(gh_ref[...], gl_ref[...], data)
    for f in range(2):
        for j in range(2):
            o_ref[rows_of(rows, f * 2 + j, 4), :] = back[
                j * rows : (j + 1) * rows, f * lanes : (f + 1) * lanes
            ]


def update_kernel(y_ref, p_ref, d_ref, ny_ref, np_ref):
    rows = y_ref.shape[1]
    for j in range(2):
        ny_ref[j] = y_ref[j] - d_ref[rows_of(rows, j, 4), :]
        np_ref[j] = p_ref[j] - d_ref[rows_of(rows, 2 + j, 4), :]


def swapped(value, distance):
    count = lax.axis_size("space")
    return lax.ppermute(value, "space", [(i, i ^ distance) for i in range(count)])


def shards(state_field, adjoint, target, initial_state, conductivity, reaction):
    steps, width_x, width_y, width_z = state_field.shape
    devices = lax.axis_size("tm")
    spaces = lax.axis_size("space")
    rows = width_x * width_y
    horizon = steps * devices
    assert steps == 2 and rows == devices and spaces == 4
    f32 = jnp.float32

    def shape(*dims):
        return jax.ShapeDtypeStruct(dims, f32)

    flat = (steps, rows, width_z)
    state_rows = state_field.reshape(flat)
    adjoint_rows = adjoint.reshape(flat)
    packed, material = pl.pallas_call(
        pack_kernel,
        out_shape=(
            shape(rows * 6, width_z),
            shape(2, width_x, width_y, width_z),
        ),
        in_specs=[hbm()] * 5,
        out_specs=(vmem(), vmem()),
        scratch_shapes=[pltpu.VMEM(flat, f32)] * 3 + [pltpu.SemaphoreType.DMA((5,))],
        name="pack",
    )(conductivity, reaction, state_rows, adjoint_rows, target.reshape(flat))
    table, twist = solver_table(horizon, devices)
    material_core = swapped(material, 1)
    material_far = swapped(material, 2)
    by_cell = lax.all_to_all(
        packed.reshape(rows * 3, 2, width_z), "tm", 0, 0, tiled=True
    ).reshape(packed.shape)
    material_both = swapped(material_far, 1)
    forward, inverse = (halves(jnp.asarray(each)) for each in time_tables(horizon, devices))
    hat = pl.pallas_call(
        forward_kernel,
        out_shape=shape(devices * 8, width_z),
        in_specs=[vmem()] * 4,
        out_specs=vmem(),
        compiler_params=grant,
        name="forward",
    )(*forward, initial_state.reshape(rows, width_z), by_cell)
    grid = (spaces * width_x, 2, width_y // 2, width_z)
    pairs = (spaces * width_x, width_y // 2, width_z)
    faces = pl.pallas_call(
        functools.partial(faces_kernel, devices),
        out_shape=(shape(*grid),) + (shape(*pairs),) * 3 + (shape(*grid),) * 5,
        in_specs=[vmem()] * 5,
        out_specs=(vmem(),) * 9,
        scratch_shapes=[pltpu.VMEM((spaces, 2, width_x, width_y, width_z), f32)],
        compiler_params=grant,
        name="faces",
    )(jnp.asarray(table), material, material_core, material_far, material_both)
    hat, faces = lax.optimization_barrier((hat, faces))
    everyone = ("space", "tm")
    by_item = lax.all_to_all(hat, everyone, 0, 0, tiled=True)
    solved = pl.pallas_call(
        functools.partial(solve_kernel, devices),
        out_shape=shape(rows * 8, width_z),
        in_specs=[vmem()] * 11,
        out_specs=vmem(),
        scratch_shapes=[pltpu.VMEM(grid, f32)] * 4,
        compiler_params=grant,
        name="solve",
    )(jnp.asarray(table), *faces, by_item)
    by_row = lax.all_to_all(solved, everyone, 0, 0, tiled=True)
    delta = pl.pallas_call(
        inverse_kernel,
        out_shape=shape(devices * 4, width_z),
        in_specs=[vmem()] * 4,
        out_specs=vmem(),
        compiler_params=grant,
        name="inverse",
    )(*inverse, jnp.asarray(twist_block(twist)), by_row)
    by_time = lax.all_to_all(delta, "tm", 0, 0, tiled=True)
    new_state, new_adjoint = pl.pallas_call(
        update_kernel,
        out_shape=(shape(*flat), shape(*flat)),
        in_specs=[vmem()] * 3,
        out_specs=(vmem(), vmem()),
        compiler_params=grant,
        name="update",
    )(state_rows, adjoint_rows, by_time)
    return new_state.reshape(state_field.shape), new_adjoint.reshape(adjoint.shape)


def solution(mesh):
    in_specs = (
        P("tm", "space", None, None),
        P("tm", "space", None, None),
        P("tm", "space", None, None),
        P("space", None, None),
        P("space", None, None),
        P("space", None, None),
    )
    out_specs = (P("tm", "space", None, None), P("tm", "space", None, None))
    return jax.shard_map(
        shards, mesh=mesh, in_specs=in_specs, out_specs=out_specs, check_vma=False
    )
```

```python
import functools

import jax
import jax.numpy as jnp
import numpy as np
from jax import lax
from jax.experimental import pallas as pl
from jax.experimental.pallas import tpu as pltpu
from jax.sharding import PartitionSpec as P


CHEB = 8
step_rate = 2.0
coupling = 1.0
lower_edge = 0.05
upper_edge = 7.0
COEF = 16
vmem = functools.partial(pl.BlockSpec, memory_space=pltpu.VMEM)
grant = pltpu.CompilerParams(vmem_limit_bytes=8 * 1024 * 1024)
hbm = functools.partial(pl.BlockSpec, memory_space=pltpu.HBM)


def time_tables(horizon, slots):
    k = np.arange(slots)[:, None]
    n = np.concatenate([np.arange(0, horizon, 2), np.arange(1, horizon, 2)])[None, :]
    angle = 2.0 * np.pi / horizon * ((k * n) % horizon)
    cosine, sine = np.cos(angle), np.sin(angle)
    alternation = np.where(n % 2 == 0, 1.0, -1.0)
    forward = np.concatenate([cosine, np.where(k == 0, alternation, -sine)], 0)
    inverse = (
        np.concatenate(
            [
                np.where(k == 0, 1.0, 2.0) * cosine,
                np.where(k == 0, alternation, -2.0 * sine),
            ],
            0,
        )
        / horizon
    )
    return forward.astype(np.float32), inverse.T.astype(np.float32)


def solver_table(horizon, slots):
    theta = 2.0 * np.pi / horizon * np.arange(slots + 1)
    shift = step_rate * (1.0 - np.cos(theta))
    twist = step_rate * np.sin(theta)
    twist[slots] = 0.0
    spread = twist * twist + coupling
    lower = (lower_edge + shift) ** 2 + spread
    upper = (upper_edge + shift) ** 2 + spread
    centre = 0.5 * (upper + lower)
    half = 0.5 * (upper - lower)
    ratio = centre / half
    gamma = np.sqrt(2.0 / half)
    offset = np.sqrt(2.0 * (centre - spread) / half)
    table = np.zeros((slots + 1, COEF))
    table[:, 0] = gamma
    table[:, 1] = offset
    table[:, 2] = shift
    table[:, 3] = 1.0 / gamma
    table[:, 4] = offset / gamma
    nodes = np.pi * (np.arange(CHEB) + 0.5) / CHEB
    points = np.cos(nodes)[None, :]
    value = centre[:, None] + half[:, None] * points
    top = np.cosh(CHEB * np.arccosh(ratio))[:, None]
    samples = (1.0 - np.cos(CHEB * np.arccos(-points)) / top) / value
    for j in range(CHEB):
        weight = (1.0 if j == 0 else 2.0) / CHEB
        table[:, 5 + j] = weight * np.sum(samples * np.cos(j * nodes)[None, :], 1)
    rows = np.broadcast_to(table.reshape(-1, 1), (table.size, 128))
    return rows.astype(np.float32), twist[:slots]


def twist_block(twist):
    block = np.zeros((twist.shape[0], 128), np.float32)
    block[:, 0] = twist
    return block


def rows_of(count, start, stride):
    return pl.ds(start, count, stride=stride)


def pack_kernel(c_hbm, r_hbm, y_hbm, p_hbm, t_hbm, o_ref, m_ref, y_ref, p_ref, t_ref, sem):
    copies = [
        pltpu.make_async_copy(source, target, sem.at[i])
        for i, (source, target) in enumerate(
            (
                (y_hbm, y_ref),
                (p_hbm, p_ref),
                (t_hbm, t_ref),
                (c_hbm, m_ref.at[0]),
                (r_hbm, m_ref.at[1]),
            )
        )
    ]
    for copy in copies:
        copy.start()
    for copy in copies:
        copy.wait()
    rows = y_ref.shape[1]
    for i, ref in enumerate((y_ref, p_ref, t_ref)):
        for j in range(2):
            o_ref[rows_of(rows, 2 * i + j, 6), :] = ref[j]


def halves(value):
    high = value.astype(jnp.bfloat16)
    return high, (value - high.astype(jnp.float32)).astype(jnp.bfloat16)


def product(high, low, data):
    data_high, data_low = halves(data)
    dot = functools.partial(lax.dot, preferred_element_type=jnp.float32)
    return dot(high, data_high) + (dot(high, data_low) + dot(low, data_high))


def forward_kernel(fh_ref, fl_ref, init_ref, x_ref, o_ref):
    rows = x_ref.shape[0] // 6
    lanes = x_ref.shape[1]
    mine = lax.axis_index("tm")
    y0, y1, p0, p1, t0, t1 = (x_ref[rows_of(rows, i, 6), :] for i in range(6))
    g0, g1 = (y * y * y * (1.0 / 3.0) + coupling * p for y, p in ((y0, p0), (y1, p1)))
    h0, h1 = (y * y * p - y + t for y, p, t in ((y0, p0, t0), (y1, p1, t1)))
    row = lax.broadcasted_iota(jnp.int32, (rows, lanes), 0)
    before = jnp.where(row == 0, init_ref[pl.ds(mine, 1), :], pltpu.roll(y1, 1, 0))
    after = jnp.where(row == rows - 1, 0.0, pltpu.roll(p0, rows - 1, 0))
    a0 = g0 + step_rate * (y0 - before)
    a1 = g1 + step_rate * (y1 - y0)
    b0 = h0 + step_rate * (p0 - p1)
    b1 = h1 + step_rate * (p1 - after)
    data = jnp.concatenate(
        [
            jnp.concatenate([a0, b0, y0, p0], 1),
            jnp.concatenate([a1, b1, y1, p1], 1),
        ],
        0,
    )
    hat = product(fh_ref[...], fl_ref[...], data)
    for f in range(2):
        for r in range(2):
            for q in range(2):
                column = (q * 2 + f) * lanes
                o_ref[rows_of(rows, (f * 2 + r) * 2 * rows + q, 2), :] = hat[
                    r * rows : (r + 1) * rows, column : column + lanes
                ]


def coefficients(co_ref, slots, subs):
    slot = lax.axis_index("tm")
    item = lax.axis_index("space")
    base = jnp.where((slot == 0) & (item % 2 == 1), slots, slot) * COEF
    lanes = co_ref.shape[1]
    return item, lambda j: jnp.broadcast_to(co_ref[pl.ds(base + j, 1), :], (subs, lanes))


def faces_kernel(
    slots,
    co_ref,
    m0_ref,
    m1_ref,
    m2_ref,
    m3_ref,
    cx,
    cy,
    cy_next,
    cy_last,
    cz_next,
    cz_last,
    bare,
    plus,
    minus,
    mat,
):
    item, coefficient = coefficients(co_ref, slots, cx.shape[2])
    gamma, offset, shift = (coefficient(j) for j in range(3))
    for piece, ref in enumerate((m0_ref, m1_ref, m2_ref, m3_ref)):
        mat[item ^ piece] = ref[...]
    count, _, subs, lanes = cx.shape
    width = mat.shape[2]
    sub = lax.broadcasted_iota(jnp.int32, (subs, lanes), 0)
    lane = lax.broadcasted_iota(jnp.int32, (subs, lanes), 1)
    first, last = sub == 0, sub == subs - 1
    left, right = lane == 0, lane == lanes - 1

    def part(which, x, parity):
        return mat.at[x // width, which, x % width][rows_of(subs, parity, 2), :]

    for x in range(count):
        even, odd = part(0, x, 0), part(0, x, 1)
        pair = 0.5 * (even + odd)
        after = 0.5 * odd + jnp.where(last, 0.0, 0.5 * pltpu.roll(even, subs - 1, 0))
        before = 0.5 * even + jnp.where(first, 0.0, 0.5 * pltpu.roll(odd, 1, 0))
        cy[x] = gamma * pair
        cy_next[x] = gamma * jnp.where(last, 0.0, after)
        cy_last[x] = gamma * jnp.where(first, 0.0, before)
        for parity, (c, side) in enumerate(((even, before), (odd, after))):
            half = 0.5 * c
            up = half + 0.5 * part(0, x + 1, parity) if x + 1 < count else half
            down = half + 0.5 * part(0, x - 1, parity) if x > 0 else half
            zn = half + jnp.where(right, 0.0, 0.5 * pltpu.roll(c, lanes - 1, 1))
            zl = half + jnp.where(left, 0.0, 0.5 * pltpu.roll(c, 1, 1))
            cx[x, parity] = gamma * up
            cz_next[x, parity] = gamma * jnp.where(right, 0.0, zn)
            cz_last[x, parity] = gamma * jnp.where(left, 0.0, zl)
            total = (up + down) + (pair + side) + (zn + zl)
            bare[x, parity] = gamma * total
            full = gamma * (total + part(1, x, parity) + shift)
            plus[x, parity] = full + offset
            minus[x, parity] = full - offset


def solve_kernel(
    slots,
    co_ref,
    cx,
    cy,
    cy_next,
    cy_last,
    cz_next,
    cz_last,
    bare,
    plus,
    minus,
    x_ref,
    o_ref,
    res,
    b0,
    b1,
    t,
):
    count, _, subs, lanes = cx.shape
    coefficient = coefficients(co_ref, slots, subs)[1]
    cells = x_ref.shape[0] // 8
    line = 2 * subs
    width = cells // line

    def place(x, parity, field):
        start = (x // width * cells + x % width * line + parity) * 2 + field
        return rows_of(subs, start, 4)

    def sweep(load, diag, emit):
        now, cx_now = load(0), None
        last = cx_last = None
        for x in range(count):
            after = load(x + 1) if x + 1 < count else None
            cx_now = (cx[x, 0], cx[x, 1]) if x + 1 < count else None
            pair = cy[x]
            side = (
                pair * now[1] + cy_last[x] * pltpu.roll(now[1], 1, 0),
                pair * now[0] + cy_next[x] * pltpu.roll(now[0], subs - 1, 0),
            )
            for parity in range(2):
                v = now[parity]
                out = diag[x, parity] * v - side[parity]
                lateral = cz_next[x, parity] * pltpu.roll(v, lanes - 1, 1)
                lateral = lateral + cz_last[x, parity] * pltpu.roll(v, 1, 1)
                if after is not None:
                    out = out - cx_now[parity] * after[parity]
                if last is not None:
                    lateral = lateral + cx_last[parity] * last[parity]
                emit(x, parity, out - lateral, v)
            last, now, cx_last = now, after, cx_now

    def kept(ref):
        return lambda x: (ref[x, 0], ref[x, 1])

    inverse_gamma = coefficient(3)
    top = coefficient(5 + CHEB - 1)

    def begin(x, parity, out, v):
        r = x_ref[place(x, parity, 0), :] + inverse_gamma * out
        res[x, parity] = r
        b0[x, parity] = top * r
        b1[x, parity] = jnp.zeros_like(r)

    sweep(
        lambda x: (x_ref[place(x, 0, 1), :], x_ref[place(x, 1, 1), :]),
        bare,
        begin,
    )

    def first_factor(source):
        def keep(x, parity, out, v):
            t[x, parity] = out

        sweep(kept(source), plus, keep)

    def clenshaw(source, target, weight):
        def keep(x, parity, out, v):
            target[x, parity] = (weight * res[x, parity] - target[x, parity]) + out

        first_factor(source)
        sweep(kept(t), minus, keep)

    def two_steps(i, carry):
        at = 5 + CHEB - 2 - 2 * i
        clenshaw(b0, b1, coefficient(at))
        clenshaw(b1, b0, coefficient(at - 1))
        return carry

    lax.fori_loop(0, (CHEB - 2) // 2, two_steps, 0)
    weight = coefficient(5)
    offset = coefficient(4)

    def finish(x, parity, out, v):
        w = (weight * res[x, parity] - b1[x, parity]) + 0.5 * out
        b1[x, parity] = w
        o_ref[place(x, parity, 0), :] = w

    first_factor(b0)
    sweep(kept(t), minus, finish)

    def image(x, parity, out, v):
        o_ref[place(x, parity, 1), :] = inverse_gamma * out - offset * v

    sweep(kept(b1), plus, image)


def inverse_kernel(gh_ref, gl_ref, b_ref, x_ref, o_ref):
    rows = x_ref.shape[0] // 8
    lanes = x_ref.shape[1]
    b = jnp.broadcast_to(b_ref[:, 0:1], (rows, lanes))
    u_re, ku_re, u_im, ku_im, v_re, kv_re, v_im, kv_im = (
        x_ref[rows_of(rows, i // 2 * 2 * rows + i % 2, 2), :] for i in range(8)
    )
    c00 = ku_re - (coupling * v_re - b * u_im)
    c01 = ku_im - (coupling * v_im + b * u_re)
    c10 = kv_re - (b * v_im - u_re)
    c11 = kv_im + (b * v_re + u_im)
    data = jnp.concatenate(
        [jnp.concatenate([c00, c10], 1), jnp.concatenate([c01, c11], 1)],
        0,
    )
    back = product(gh_ref[...], gl_ref[...], data)
    for f in range(2):
        for j in range(2):
            o_ref[rows_of(rows, f * 2 + j, 4), :] = back[
                j * rows : (j + 1) * rows, f * lanes : (f + 1) * lanes
            ]


def update_kernel(y_ref, p_ref, d_ref, ny_ref, np_ref):
    rows = y_ref.shape[1]
    for j in range(2):
        ny_ref[j] = y_ref[j] - d_ref[rows_of(rows, j, 4), :]
        np_ref[j] = p_ref[j] - d_ref[rows_of(rows, 2 + j, 4), :]


def swapped(value, distance):
    count = lax.axis_size("space")
    return lax.ppermute(value, "space", [(i, i ^ distance) for i in range(count)])


def mirrored(value, distance):
    spaces = lax.axis_size("space")
    devices = lax.axis_size("tm")
    layers = 4
    share = devices // layers
    pairs = []
    for tm in range(devices):
        other = (layers - 1 - tm // share) * share + tm % share
        pairs += [(tm * spaces + i, other * spaces + (i ^ distance)) for i in range(spaces)]
    return lax.ppermute(value, ("tm", "space"), pairs)


def shards(state_field, adjoint, target, initial_state, conductivity, reaction):
    steps, width_x, width_y, width_z = state_field.shape
    devices = lax.axis_size("tm")
    spaces = lax.axis_size("space")
    rows = width_x * width_y
    horizon = steps * devices
    assert steps == 2 and rows == devices and spaces == 4
    f32 = jnp.float32

    def shape(*dims):
        return jax.ShapeDtypeStruct(dims, f32)

    flat = (steps, rows, width_z)
    state_rows = state_field.reshape(flat)
    adjoint_rows = adjoint.reshape(flat)
    packed, material = pl.pallas_call(
        pack_kernel,
        out_shape=(
            shape(rows * 6, width_z),
            shape(2, width_x, width_y, width_z),
        ),
        in_specs=[hbm()] * 5,
        out_specs=(vmem(), vmem()),
        scratch_shapes=[pltpu.VMEM(flat, f32)] * 3 + [pltpu.SemaphoreType.DMA((5,))],
        compiler_params=grant,
        name="pack",
    )(
        *(
            pltpu.with_memory_space_constraint(each, pltpu.HBM)
            for each in (
                conductivity,
                reaction,
                state_rows,
                adjoint_rows,
                target.reshape(flat),
            )
        )
    )
    table, twist = solver_table(horizon, devices)
    material_core = swapped(material, 1)
    material_far = mirrored(material, 2)
    by_cell = lax.all_to_all(
        packed.reshape(rows * 3, 2, width_z), "tm", 0, 0, tiled=True
    ).reshape(packed.shape)
    material_both = swapped(material_far, 1)
    forward, inverse = (halves(jnp.asarray(each)) for each in time_tables(horizon, devices))
    hat = pl.pallas_call(
        forward_kernel,
        out_shape=shape(devices * 8, width_z),
        in_specs=[vmem()] * 4,
        out_specs=vmem(),
        compiler_params=grant,
        name="forward",
    )(*forward, initial_state.reshape(rows, width_z), by_cell)
    grid = (spaces * width_x, 2, width_y // 2, width_z)
    pairs = (spaces * width_x, width_y // 2, width_z)
    faces = pl.pallas_call(
        functools.partial(faces_kernel, devices),
        out_shape=(shape(*grid),) + (shape(*pairs),) * 3 + (shape(*grid),) * 5,
        in_specs=[vmem()] * 5,
        out_specs=(vmem(),) * 9,
        scratch_shapes=[pltpu.VMEM((spaces, 2, width_x, width_y, width_z), f32)],
        compiler_params=grant,
        name="faces",
    )(jnp.asarray(table), material, material_core, material_far, material_both)
    hat, faces = lax.optimization_barrier((hat, faces))
    everyone = ("space", "tm")
    by_item = lax.all_to_all(hat, everyone, 0, 0, tiled=True)
    solved = pl.pallas_call(
        functools.partial(solve_kernel, devices),
        out_shape=shape(rows * 8, width_z),
        in_specs=[vmem()] * 11,
        out_specs=vmem(),
        scratch_shapes=[pltpu.VMEM(grid, f32)] * 4,
        compiler_params=grant,
        name="solve",
    )(jnp.asarray(table), *faces, by_item)
    by_row = lax.all_to_all(solved, everyone, 0, 0, tiled=True)
    delta = pl.pallas_call(
        inverse_kernel,
        out_shape=shape(devices * 4, width_z),
        in_specs=[vmem()] * 4,
        out_specs=vmem(),
        compiler_params=grant,
        name="inverse",
    )(*inverse, jnp.asarray(twist_block(twist)), by_row)
    by_time = lax.all_to_all(delta, "tm", 0, 0, tiled=True)
    new_state, new_adjoint = pl.pallas_call(
        update_kernel,
        out_shape=(shape(*flat), shape(*flat)),
        in_specs=[vmem()] * 3,
        out_specs=(vmem(), vmem()),
        compiler_params=grant,
        name="update",
    )(state_rows, adjoint_rows, by_time)
    return new_state.reshape(state_field.shape), new_adjoint.reshape(adjoint.shape)


def solution(mesh):
    in_specs = (
        P("tm", "space", None, None),
        P("tm", "space", None, None),
        P("tm", "space", None, None),
        P("space", None, None),
        P("space", None, None),
        P("space", None, None),
    )
    out_specs = (P("tm", "space", None, None), P("tm", "space", None, None))
    return jax.shard_map(
        shards, mesh=mesh, in_specs=in_specs, out_specs=out_specs, check_vma=False
    )
```

```python
import functools

import jax
import jax.numpy as jnp
import numpy as np
from jax import lax
from jax.experimental import pallas as pl
from jax.experimental.pallas import tpu as pltpu
from jax.sharding import PartitionSpec as P


CHEB = 8
step_rate = 2.0
coupling = 1.0
lower_edge = 0.05
upper_edge = 7.0
COEF = 16
vmem = functools.partial(pl.BlockSpec, memory_space=pltpu.VMEM)
grant = pltpu.CompilerParams(vmem_limit_bytes=8 * 1024 * 1024)
hbm = functools.partial(pl.BlockSpec, memory_space=pltpu.HBM)


def time_tables(horizon, slots):
    k = np.arange(slots)[:, None]
    n = np.concatenate([np.arange(0, horizon, 2), np.arange(1, horizon, 2)])[None, :]
    angle = 2.0 * np.pi / horizon * ((k * n) % horizon)
    cosine, sine = np.cos(angle), np.sin(angle)
    alternation = np.where(n % 2 == 0, 1.0, -1.0)
    forward = np.concatenate([cosine, np.where(k == 0, alternation, -sine)], 0)
    inverse = (
        np.concatenate(
            [
                np.where(k == 0, 1.0, 2.0) * cosine,
                np.where(k == 0, alternation, -2.0 * sine),
            ],
            0,
        )
        / horizon
    )
    return forward.astype(np.float32), inverse.T.astype(np.float32)


def solver_table(horizon, slots):
    theta = 2.0 * np.pi / horizon * np.arange(slots + 1)
    shift = step_rate * (1.0 - np.cos(theta))
    twist = step_rate * np.sin(theta)
    twist[slots] = 0.0
    spread = twist * twist + coupling
    lower = (lower_edge + shift) ** 2 + spread
    upper = (upper_edge + shift) ** 2 + spread
    centre = 0.5 * (upper + lower)
    half = 0.5 * (upper - lower)
    ratio = centre / half
    gamma = np.sqrt(2.0 / half)
    offset = np.sqrt(2.0 * (centre - spread) / half)
    table = np.zeros((slots + 1, COEF))
    table[:, 0] = gamma
    table[:, 1] = offset
    table[:, 2] = shift
    table[:, 3] = 1.0 / gamma
    table[:, 4] = offset / gamma
    nodes = np.pi * (np.arange(CHEB) + 0.5) / CHEB
    points = np.cos(nodes)[None, :]
    value = centre[:, None] + half[:, None] * points
    top = np.cosh(CHEB * np.arccosh(ratio))[:, None]
    samples = (1.0 - np.cos(CHEB * np.arccos(-points)) / top) / value
    for j in range(CHEB):
        weight = (1.0 if j == 0 else 2.0) / CHEB
        table[:, 5 + j] = weight * np.sum(samples * np.cos(j * nodes)[None, :], 1)
    rows = np.broadcast_to(table.reshape(-1, 1), (table.size, 128))
    return rows.astype(np.float32), twist[:slots]


def twist_block(twist):
    block = np.zeros((twist.shape[0], 128), np.float32)
    block[:, 0] = twist
    return block


def rows_of(count, start, stride):
    return pl.ds(start, count, stride=stride)


def pack_kernel(c_hbm, r_hbm, y_hbm, p_hbm, t_hbm, o_hbm, m_ref, sem):
    pairs = [
        (each.at[j], o_hbm.at[:, 2 * i + j, 0, :])
        for i, each in enumerate((y_hbm, p_hbm, t_hbm))
        for j in range(2)
    ]
    pairs += [(c_hbm, m_ref.at[0]), (r_hbm, m_ref.at[1])]
    copies = [
        pltpu.make_async_copy(source, target, sem.at[i])
        for i, (source, target) in enumerate(pairs)
    ]
    for copy in copies:
        copy.start()
    for copy in copies:
        copy.wait()


def halves(value):
    high = value.astype(jnp.bfloat16)
    return high, (value - high.astype(jnp.float32)).astype(jnp.bfloat16)


def product(high, low, data):
    data_high, data_low = halves(data)
    dot = functools.partial(lax.dot, preferred_element_type=jnp.float32)
    return dot(high, data_high) + (dot(high, data_low) + dot(low, data_high))


def forward_kernel(fh_ref, fl_ref, init_ref, x_ref, o_ref):
    rows = x_ref.shape[0] // 6
    lanes = x_ref.shape[1]
    mine = lax.axis_index("tm")
    y0, y1, p0, p1, t0, t1 = (x_ref[rows_of(rows, i, 6), :] for i in range(6))
    g0, g1 = (y * y * y * (1.0 / 3.0) + coupling * p for y, p in ((y0, p0), (y1, p1)))
    h0, h1 = (y * y * p - y + t for y, p, t in ((y0, p0, t0), (y1, p1, t1)))
    row = lax.broadcasted_iota(jnp.int32, (rows, lanes), 0)
    before = jnp.where(row == 0, init_ref[pl.ds(mine, 1), :], pltpu.roll(y1, 1, 0))
    after = jnp.where(row == rows - 1, 0.0, pltpu.roll(p0, rows - 1, 0))
    a0 = g0 + step_rate * (y0 - before)
    a1 = g1 + step_rate * (y1 - y0)
    b0 = h0 + step_rate * (p0 - p1)
    b1 = h1 + step_rate * (p1 - after)
    data = jnp.concatenate(
        [
            jnp.concatenate([a0, b0, y0, p0], 1),
            jnp.concatenate([a1, b1, y1, p1], 1),
        ],
        0,
    )
    hat = product(fh_ref[...], fl_ref[...], data)
    for f in range(2):
        for r in range(2):
            for q in range(2):
                column = (q * 2 + f) * lanes
                o_ref[rows_of(rows, (f * 2 + r) * 2 * rows + q, 2), :] = hat[
                    r * rows : (r + 1) * rows, column : column + lanes
                ]


def coefficients(co_ref, slots, subs):
    slot = lax.axis_index("tm")
    item = lax.axis_index("space")
    base = jnp.where((slot == 0) & (item % 2 == 1), slots, slot) * COEF
    lanes = co_ref.shape[1]
    return item, lambda j: jnp.broadcast_to(co_ref[pl.ds(base + j, 1), :], (subs, lanes))


def faces_kernel(
    slots,
    co_ref,
    m0_ref,
    m1_ref,
    m2_ref,
    m3_ref,
    cx,
    cy,
    cy_next,
    cy_last,
    cz_next,
    cz_last,
    bare,
    plus,
    minus,
    mat,
):
    item, coefficient = coefficients(co_ref, slots, cx.shape[2])
    gamma, offset, shift = (coefficient(j) for j in range(3))
    for piece, ref in enumerate((m0_ref, m1_ref, m2_ref, m3_ref)):
        mat[item ^ piece] = ref[...]
    count, _, subs, lanes = cx.shape
    width = mat.shape[2]
    sub = lax.broadcasted_iota(jnp.int32, (subs, lanes), 0)
    lane = lax.broadcasted_iota(jnp.int32, (subs, lanes), 1)
    first, last = sub == 0, sub == subs - 1
    left, right = lane == 0, lane == lanes - 1

    def part(which, x, parity):
        return mat.at[x // width, which, x % width][rows_of(subs, parity, 2), :]

    for x in range(count):
        even, odd = part(0, x, 0), part(0, x, 1)
        pair = 0.5 * (even + odd)
        after = 0.5 * odd + jnp.where(last, 0.0, 0.5 * pltpu.roll(even, subs - 1, 0))
        before = 0.5 * even + jnp.where(first, 0.0, 0.5 * pltpu.roll(odd, 1, 0))
        cy[x] = gamma * pair
        cy_next[x] = gamma * jnp.where(last, 0.0, after)
        cy_last[x] = gamma * jnp.where(first, 0.0, before)
        for parity, (c, side) in enumerate(((even, before), (odd, after))):
            half = 0.5 * c
            up = half + 0.5 * part(0, x + 1, parity) if x + 1 < count else half
            down = half + 0.5 * part(0, x - 1, parity) if x > 0 else half
            zn = half + jnp.where(right, 0.0, 0.5 * pltpu.roll(c, lanes - 1, 1))
            zl = half + jnp.where(left, 0.0, 0.5 * pltpu.roll(c, 1, 1))
            cx[x, parity] = gamma * up
            cz_next[x, parity] = gamma * jnp.where(right, 0.0, zn)
            cz_last[x, parity] = gamma * jnp.where(left, 0.0, zl)
            total = (up + down) + (pair + side) + (zn + zl)
            bare[x, parity] = gamma * total
            full = gamma * (total + part(1, x, parity) + shift)
            plus[x, parity] = full + offset
            minus[x, parity] = full - offset


def solve_kernel(
    slots,
    co_ref,
    cx,
    cy,
    cy_next,
    cy_last,
    cz_next,
    cz_last,
    bare,
    plus,
    minus,
    x_ref,
    o_ref,
    res,
    b0,
    b1,
    t,
):
    count, _, subs, lanes = cx.shape
    coefficient = coefficients(co_ref, slots, subs)[1]
    cells = x_ref.shape[0] // 8
    line = 2 * subs
    width = cells // line

    def place(x, parity, field):
        start = (x // width * cells + x % width * line + parity) * 2 + field
        return rows_of(subs, start, 4)

    def sweep(load, diag, emit):
        now, cx_now = load(0), None
        last = cx_last = None
        for x in range(count):
            after = load(x + 1) if x + 1 < count else None
            cx_now = (cx[x, 0], cx[x, 1]) if x + 1 < count else None
            pair = cy[x]
            side = (
                pair * now[1] + cy_last[x] * pltpu.roll(now[1], 1, 0),
                pair * now[0] + cy_next[x] * pltpu.roll(now[0], subs - 1, 0),
            )
            for parity in range(2):
                v = now[parity]
                out = diag[x, parity] * v - side[parity]
                lateral = cz_next[x, parity] * pltpu.roll(v, lanes - 1, 1)
                lateral = lateral + cz_last[x, parity] * pltpu.roll(v, 1, 1)
                if after is not None:
                    out = out - cx_now[parity] * after[parity]
                if last is not None:
                    lateral = lateral + cx_last[parity] * last[parity]
                emit(x, parity, out - lateral, v)
            last, now, cx_last = now, after, cx_now

    def kept(ref):
        return lambda x: (ref[x, 0], ref[x, 1])

    inverse_gamma = coefficient(3)
    top = coefficient(5 + CHEB - 1)

    def begin(x, parity, out, v):
        r = x_ref[place(x, parity, 0), :] + inverse_gamma * out
        res[x, parity] = r
        b0[x, parity] = top * r
        b1[x, parity] = jnp.zeros_like(r)

    sweep(
        lambda x: (x_ref[place(x, 0, 1), :], x_ref[place(x, 1, 1), :]),
        bare,
        begin,
    )

    def first_factor(source):
        def keep(x, parity, out, v):
            t[x, parity] = out

        sweep(kept(source), plus, keep)

    def clenshaw(source, target, weight):
        def keep(x, parity, out, v):
            target[x, parity] = (weight * res[x, parity] - target[x, parity]) + out

        first_factor(source)
        sweep(kept(t), minus, keep)

    def two_steps(i, carry):
        at = 5 + CHEB - 2 - 2 * i
        clenshaw(b0, b1, coefficient(at))
        clenshaw(b1, b0, coefficient(at - 1))
        return carry

    lax.fori_loop(0, (CHEB - 2) // 2, two_steps, 0)
    weight = coefficient(5)
    offset = coefficient(4)

    def finish(x, parity, out, v):
        w = (weight * res[x, parity] - b1[x, parity]) + 0.5 * out
        b1[x, parity] = w
        o_ref[place(x, parity, 0), :] = w

    first_factor(b0)
    sweep(kept(t), minus, finish)

    def image(x, parity, out, v):
        o_ref[place(x, parity, 1), :] = inverse_gamma * out - offset * v

    sweep(kept(b1), plus, image)


def inverse_kernel(gh_ref, gl_ref, b_ref, x_ref, o_ref):
    rows = x_ref.shape[0] // 8
    lanes = x_ref.shape[1]
    b = jnp.broadcast_to(b_ref[:, 0:1], (rows, lanes))
    u_re, ku_re, u_im, ku_im, v_re, kv_re, v_im, kv_im = (
        x_ref[rows_of(rows, i // 2 * 2 * rows + i % 2, 2), :] for i in range(8)
    )
    c00 = ku_re - (coupling * v_re - b * u_im)
    c01 = ku_im - (coupling * v_im + b * u_re)
    c10 = kv_re - (b * v_im - u_re)
    c11 = kv_im + (b * v_re + u_im)
    data = jnp.concatenate(
        [jnp.concatenate([c00, c10], 1), jnp.concatenate([c01, c11], 1)],
        0,
    )
    back = product(gh_ref[...], gl_ref[...], data)
    for f in range(2):
        for j in range(2):
            o_ref[rows_of(rows, f * 2 + j, 4), :] = back[
                j * rows : (j + 1) * rows, f * lanes : (f + 1) * lanes
            ]


def update_kernel(y_ref, p_ref, d_ref, ny_ref, np_ref):
    rows = y_ref.shape[1]
    for j in range(2):
        ny_ref[j] = y_ref[j] - d_ref[rows_of(rows, j, 4), :]
        np_ref[j] = p_ref[j] - d_ref[rows_of(rows, 2 + j, 4), :]


def swapped(value, distance):
    count = lax.axis_size("space")
    return lax.ppermute(value, "space", [(i, i ^ distance) for i in range(count)])


def mirrored(value, distance):
    spaces = lax.axis_size("space")
    devices = lax.axis_size("tm")
    layers = 4
    share = devices // layers
    pairs = []
    for tm in range(devices):
        other = (layers - 1 - tm // share) * share + tm % share
        pairs += [(tm * spaces + i, other * spaces + (i ^ distance)) for i in range(spaces)]
    return lax.ppermute(value, ("tm", "space"), pairs)


def shards(state_field, adjoint, target, initial_state, conductivity, reaction):
    steps, width_x, width_y, width_z = state_field.shape
    devices = lax.axis_size("tm")
    spaces = lax.axis_size("space")
    rows = width_x * width_y
    horizon = steps * devices
    assert steps == 2 and rows == devices and spaces == 4
    f32 = jnp.float32

    def shape(*dims):
        return jax.ShapeDtypeStruct(dims, f32)

    flat = (steps, rows, width_z)
    state_rows = state_field.reshape(flat)
    adjoint_rows = adjoint.reshape(flat)
    packed, material = pl.pallas_call(
        pack_kernel,
        out_shape=(
            shape(rows, 6, 1, width_z),
            shape(2, width_x, width_y, width_z),
        ),
        in_specs=[hbm()] * 5,
        out_specs=(hbm(), vmem()),
        scratch_shapes=[pltpu.SemaphoreType.DMA((8,))],
        compiler_params=grant,
        name="pack",
    )(
        *(
            pltpu.with_memory_space_constraint(each, pltpu.HBM)
            for each in (
                conductivity,
                reaction,
                state_rows,
                adjoint_rows,
                target.reshape(flat),
            )
        )
    )
    table, twist = solver_table(horizon, devices)
    material_core = swapped(material, 1)
    material_far = mirrored(material, 2)
    by_cell = lax.all_to_all(
        packed.reshape(rows * 3, 2, width_z), "tm", 0, 0, tiled=True
    ).reshape(rows * 6, width_z)
    material_both = swapped(material_far, 1)
    forward, inverse = (halves(jnp.asarray(each)) for each in time_tables(horizon, devices))
    hat = pl.pallas_call(
        forward_kernel,
        out_shape=shape(devices * 8, width_z),
        in_specs=[vmem()] * 4,
        out_specs=vmem(),
        compiler_params=grant,
        name="forward",
    )(*forward, initial_state.reshape(rows, width_z), by_cell)
    grid = (spaces * width_x, 2, width_y // 2, width_z)
    pairs = (spaces * width_x, width_y // 2, width_z)
    faces = pl.pallas_call(
        functools.partial(faces_kernel, devices),
        out_shape=(shape(*grid),) + (shape(*pairs),) * 3 + (shape(*grid),) * 5,
        in_specs=[vmem()] * 5,
        out_specs=(vmem(),) * 9,
        scratch_shapes=[pltpu.VMEM((spaces, 2, width_x, width_y, width_z), f32)],
        compiler_params=grant,
        name="faces",
    )(jnp.asarray(table), material, material_core, material_far, material_both)
    hat, faces = lax.optimization_barrier((hat, faces))
    everyone = ("space", "tm")
    by_item = lax.all_to_all(hat, everyone, 0, 0, tiled=True)
    solved = pl.pallas_call(
        functools.partial(solve_kernel, devices),
        out_shape=shape(rows * 8, width_z),
        in_specs=[vmem()] * 11,
        out_specs=vmem(),
        scratch_shapes=[pltpu.VMEM(grid, f32)] * 4,
        compiler_params=grant,
        name="solve",
    )(jnp.asarray(table), *faces, by_item)
    by_row = lax.all_to_all(solved, everyone, 0, 0, tiled=True)
    delta = pl.pallas_call(
        inverse_kernel,
        out_shape=shape(devices * 4, width_z),
        in_specs=[vmem()] * 4,
        out_specs=vmem(),
        compiler_params=grant,
        name="inverse",
    )(*inverse, jnp.asarray(twist_block(twist)), by_row)
    by_time = lax.all_to_all(delta, "tm", 0, 0, tiled=True)
    new_state, new_adjoint = pl.pallas_call(
        update_kernel,
        out_shape=(shape(*flat), shape(*flat)),
        in_specs=[vmem()] * 3,
        out_specs=(vmem(), vmem()),
        compiler_params=grant,
        name="update",
    )(state_rows, adjoint_rows, by_time)
    return new_state.reshape(state_field.shape), new_adjoint.reshape(adjoint.shape)


def solution(mesh):
    in_specs = (
        P("tm", "space", None, None),
        P("tm", "space", None, None),
        P("tm", "space", None, None),
        P("space", None, None),
        P("space", None, None),
        P("space", None, None),
    )
    out_specs = (P("tm", "space", None, None), P("tm", "space", None, None))
    return jax.shard_map(
        shards, mesh=mesh, in_specs=in_specs, out_specs=out_specs, check_vma=False
    )
```

```python
import functools

import jax
import jax.numpy as jnp
import numpy as np
from jax import lax
from jax.experimental import pallas as pl
from jax.experimental.pallas import tpu as pltpu
from jax.sharding import Mesh
from jax.sharding import PartitionSpec as P


CHEB = 8
LAYERS = 4
SIDE = 4
LINES = ("zl", "x", "y")
step_rate = 2.0
coupling = 1.0
lower_edge = 0.05
upper_edge = 7.0
COEF = 16
vmem = functools.partial(pl.BlockSpec, memory_space=pltpu.VMEM)
grant = pltpu.CompilerParams(vmem_limit_bytes=8 * 1024 * 1024)
hbm = functools.partial(pl.BlockSpec, memory_space=pltpu.HBM)


def time_tables(horizon, slots):
    k = np.arange(slots)[:, None]
    times = np.arange(slots).reshape(LAYERS, SIDE, SIDE).transpose(0, 2, 1).reshape(-1)
    n = np.concatenate([2 * times, 2 * times + 1])[None, :]
    angle = 2.0 * np.pi / horizon * ((k * n) % horizon)
    cosine, sine = np.cos(angle), np.sin(angle)
    alternation = np.where(n % 2 == 0, 1.0, -1.0)
    forward = np.concatenate([cosine, np.where(k == 0, alternation, -sine)], 0)
    inverse = (
        np.concatenate(
            [
                np.where(k == 0, 1.0, 2.0) * cosine,
                np.where(k == 0, alternation, -2.0 * sine),
            ],
            0,
        )
        / horizon
    )
    return forward.astype(np.float32), inverse.T.astype(np.float32)


def solver_table(horizon, slots):
    theta = 2.0 * np.pi / horizon * np.arange(slots + 1)
    shift = step_rate * (1.0 - np.cos(theta))
    twist = step_rate * np.sin(theta)
    twist[slots] = 0.0
    spread = twist * twist + coupling
    lower = (lower_edge + shift) ** 2 + spread
    upper = (upper_edge + shift) ** 2 + spread
    centre = 0.5 * (upper + lower)
    half = 0.5 * (upper - lower)
    ratio = centre / half
    gamma = np.sqrt(2.0 / half)
    offset = np.sqrt(2.0 * (centre - spread) / half)
    table = np.zeros((slots + 1, COEF))
    table[:, 0] = gamma
    table[:, 1] = offset
    table[:, 2] = shift
    table[:, 3] = 1.0 / gamma
    table[:, 4] = offset / gamma
    nodes = np.pi * (np.arange(CHEB) + 0.5) / CHEB
    points = np.cos(nodes)[None, :]
    value = centre[:, None] + half[:, None] * points
    top = np.cosh(CHEB * np.arccosh(ratio))[:, None]
    samples = (1.0 - np.cos(CHEB * np.arccos(-points)) / top) / value
    for j in range(CHEB):
        weight = (1.0 if j == 0 else 2.0) / CHEB
        table[:, 5 + j] = weight * np.sum(samples * np.cos(j * nodes)[None, :], 1)
    rows = np.broadcast_to(table.reshape(-1, 1), (table.size, 128))
    return rows.astype(np.float32), twist[:slots]


def twist_block(twist):
    block = np.zeros((twist.shape[0], 128), np.float32)
    block[:, 0] = twist
    return block


def line_index():
    zl, x, y = (lax.axis_index(each) for each in LINES)
    return (zl * SIDE + x) * SIDE + y


def rows_of(count, start, stride):
    return pl.ds(start, count, stride=stride)


def pack_kernel(c_hbm, r_hbm, y_hbm, p_hbm, t_hbm, o_hbm, m_ref, lines, sem, out_sem):
    pairs = [
        (each.at[j], lines.at[:, 2 * i + j, 0, :])
        for i, each in enumerate((y_hbm, p_hbm, t_hbm))
        for j in range(2)
    ]
    pairs += [(c_hbm, m_ref.at[0]), (r_hbm, m_ref.at[1])]
    copies = [
        pltpu.make_async_copy(source, target, sem.at[i])
        for i, (source, target) in enumerate(pairs)
    ]
    for copy in copies:
        copy.start()
    for copy in copies[:6]:
        copy.wait()
    out = pltpu.make_async_copy(lines, o_hbm, out_sem)
    out.start()
    for copy in copies[6:]:
        copy.wait()
    out.wait()


def halves(value):
    high = value.astype(jnp.bfloat16)
    return high, (value - high.astype(jnp.float32)).astype(jnp.bfloat16)


def product(high, low, data):
    data_high, data_low = halves(data)
    dot = functools.partial(lax.dot, preferred_element_type=jnp.float32)
    return dot(high, data_high) + (dot(high, data_low) + dot(low, data_high))


def forward_kernel(fh_ref, fl_ref, init_ref, x_ref, o_ref):
    rows = x_ref.shape[0] // 6
    lanes = x_ref.shape[1]
    mine = line_index()
    y0, y1, p0, p1, t0, t1 = (x_ref[rows_of(rows, i, 6), :] for i in range(6))
    g0, g1 = (y * y * y * (1.0 / 3.0) + coupling * p for y, p in ((y0, p0), (y1, p1)))
    h0, h1 = (y * y * p - y + t for y, p, t in ((y0, p0, t0), (y1, p1, t1)))
    row = lax.broadcasted_iota(jnp.int32, (rows, lanes), 0)
    across, down = row // SIDE % SIDE, row % SIDE
    jump = SIDE * (SIDE - 1) - 1
    before = jnp.where(
        across > 0,
        pltpu.roll(y1, SIDE, 0),
        jnp.where(down > 0, pltpu.roll(y1, rows - jump, 0), pltpu.roll(y1, 1, 0)),
    )
    before = jnp.where(row == 0, init_ref[pl.ds(mine, 1), :], before)
    after = jnp.where(
        across < SIDE - 1,
        pltpu.roll(p0, rows - SIDE, 0),
        jnp.where(down < SIDE - 1, pltpu.roll(p0, jump, 0), pltpu.roll(p0, rows - 1, 0)),
    )
    after = jnp.where(row == rows - 1, 0.0, after)
    a0 = g0 + step_rate * (y0 - before)
    a1 = g1 + step_rate * (y1 - y0)
    b0 = h0 + step_rate * (p0 - p1)
    b1 = h1 + step_rate * (p1 - after)
    data = jnp.concatenate(
        [
            jnp.concatenate([a0, b0, y0, p0], 1),
            jnp.concatenate([a1, b1, y1, p1], 1),
        ],
        0,
    )
    hat = product(fh_ref[...], fl_ref[...], data)
    for f in range(2):
        for r in range(2):
            for q in range(2):
                column = (q * 2 + f) * lanes
                o_ref[rows_of(rows, (f * 2 + r) * 2 * rows + q, 2), :] = hat[
                    r * rows : (r + 1) * rows, column : column + lanes
                ]


def coefficients(co_ref, slots, subs):
    slot = line_index()
    item = lax.axis_index("space")
    base = jnp.where((slot == 0) & (item % 2 == 1), slots, slot) * COEF
    lanes = co_ref.shape[1]
    return item, lambda j: jnp.broadcast_to(co_ref[pl.ds(base + j, 1), :], (subs, lanes))


def faces_kernel(
    slots,
    co_ref,
    m0_ref,
    m1_ref,
    m2_ref,
    m3_ref,
    cx,
    cy,
    cy_next,
    cy_last,
    cz_next,
    cz_last,
    bare,
    plus,
    minus,
    mat,
):
    item, coefficient = coefficients(co_ref, slots, cx.shape[2])
    gamma, offset, shift = (coefficient(j) for j in range(3))
    for piece, ref in enumerate((m0_ref, m1_ref, m2_ref, m3_ref)):
        mat[item ^ piece] = ref[...]
    count, _, subs, lanes = cx.shape
    width = mat.shape[2]
    sub = lax.broadcasted_iota(jnp.int32, (subs, lanes), 0)
    lane = lax.broadcasted_iota(jnp.int32, (subs, lanes), 1)
    first, last = sub == 0, sub == subs - 1
    left, right = lane == 0, lane == lanes - 1

    def part(which, x, parity):
        return mat.at[x // width, which, x % width][rows_of(subs, parity, 2), :]

    for x in range(count):
        even, odd = part(0, x, 0), part(0, x, 1)
        pair = 0.5 * (even + odd)
        after = 0.5 * odd + jnp.where(last, 0.0, 0.5 * pltpu.roll(even, subs - 1, 0))
        before = 0.5 * even + jnp.where(first, 0.0, 0.5 * pltpu.roll(odd, 1, 0))
        cy[x] = gamma * pair
        cy_next[x] = gamma * jnp.where(last, 0.0, after)
        cy_last[x] = gamma * jnp.where(first, 0.0, before)
        for parity, (c, side) in enumerate(((even, before), (odd, after))):
            half = 0.5 * c
            up = half + 0.5 * part(0, x + 1, parity) if x + 1 < count else half
            down = half + 0.5 * part(0, x - 1, parity) if x > 0 else half
            zn = half + jnp.where(right, 0.0, 0.5 * pltpu.roll(c, lanes - 1, 1))
            zl = half + jnp.where(left, 0.0, 0.5 * pltpu.roll(c, 1, 1))
            cx[x, parity] = gamma * up
            cz_next[x, parity] = gamma * jnp.where(right, 0.0, zn)
            cz_last[x, parity] = gamma * jnp.where(left, 0.0, zl)
            total = (up + down) + (pair + side) + (zn + zl)
            bare[x, parity] = gamma * total
            full = gamma * (total + part(1, x, parity) + shift)
            plus[x, parity] = full + offset
            minus[x, parity] = full - offset


def solve_kernel(
    slots,
    co_ref,
    cx,
    cy,
    cy_next,
    cy_last,
    cz_next,
    cz_last,
    bare,
    plus,
    minus,
    x_ref,
    o_ref,
    res,
    b0,
    b1,
    t,
):
    count, _, subs, lanes = cx.shape
    coefficient = coefficients(co_ref, slots, subs)[1]
    cells = x_ref.shape[0] // 8
    line = 2 * subs
    width = cells // line

    def place(x, parity, field):
        start = (x // width * cells + x % width * line + parity) * 2 + field
        return rows_of(subs, start, 4)

    def sweep(load, diag, emit):
        now, cx_now = load(0), None
        last = cx_last = None
        for x in range(count):
            after = load(x + 1) if x + 1 < count else None
            cx_now = (cx[x, 0], cx[x, 1]) if x + 1 < count else None
            pair = cy[x]
            side = (
                pair * now[1] + cy_last[x] * pltpu.roll(now[1], 1, 0),
                pair * now[0] + cy_next[x] * pltpu.roll(now[0], subs - 1, 0),
            )
            for parity in range(2):
                v = now[parity]
                out = diag[x, parity] * v - side[parity]
                lateral = cz_next[x, parity] * pltpu.roll(v, lanes - 1, 1)
                lateral = lateral + cz_last[x, parity] * pltpu.roll(v, 1, 1)
                if after is not None:
                    out = out - cx_now[parity] * after[parity]
                if last is not None:
                    lateral = lateral + cx_last[parity] * last[parity]
                emit(x, parity, out - lateral, v)
            last, now, cx_last = now, after, cx_now

    def kept(ref):
        return lambda x: (ref[x, 0], ref[x, 1])

    inverse_gamma = coefficient(3)
    top = coefficient(5 + CHEB - 1)

    def begin(x, parity, out, v):
        r = x_ref[place(x, parity, 0), :] + inverse_gamma * out
        res[x, parity] = r
        b0[x, parity] = top * r
        b1[x, parity] = jnp.zeros_like(r)

    sweep(
        lambda x: (x_ref[place(x, 0, 1), :], x_ref[place(x, 1, 1), :]),
        bare,
        begin,
    )

    def first_factor(source):
        def keep(x, parity, out, v):
            t[x, parity] = out

        sweep(kept(source), plus, keep)

    def clenshaw(source, target, weight):
        def keep(x, parity, out, v):
            target[x, parity] = (weight * res[x, parity] - target[x, parity]) + out

        first_factor(source)
        sweep(kept(t), minus, keep)

    def two_steps(i, carry):
        at = 5 + CHEB - 2 - 2 * i
        clenshaw(b0, b1, coefficient(at))
        clenshaw(b1, b0, coefficient(at - 1))
        return carry

    lax.fori_loop(0, (CHEB - 2) // 2, two_steps, 0)
    weight = coefficient(5)
    offset = coefficient(4)

    def finish(x, parity, out, v):
        w = (weight * res[x, parity] - b1[x, parity]) + 0.5 * out
        b1[x, parity] = w
        o_ref[place(x, parity, 0), :] = w

    first_factor(b0)
    sweep(kept(t), minus, finish)

    def image(x, parity, out, v):
        o_ref[place(x, parity, 1), :] = inverse_gamma * out - offset * v

    sweep(kept(b1), plus, image)


def inverse_kernel(gh_ref, gl_ref, b_ref, x_ref, o_ref):
    rows = x_ref.shape[0] // 8
    lanes = x_ref.shape[1]
    b = jnp.broadcast_to(b_ref[:, 0:1], (rows, lanes))
    u_re, ku_re, u_im, ku_im, v_re, kv_re, v_im, kv_im = (
        x_ref[rows_of(rows, i // 2 * 2 * rows + i % 2, 2), :] for i in range(8)
    )
    c00 = ku_re - (coupling * v_re - b * u_im)
    c01 = ku_im - (coupling * v_im + b * u_re)
    c10 = kv_re - (b * v_im - u_re)
    c11 = kv_im + (b * v_re + u_im)
    data = jnp.concatenate(
        [jnp.concatenate([c00, c10], 1), jnp.concatenate([c01, c11], 1)],
        0,
    )
    back = product(gh_ref[...], gl_ref[...], data)
    for f in range(2):
        for j in range(2):
            o_ref[rows_of(rows, f * 2 + j, 4), :] = back[
                j * rows : (j + 1) * rows, f * lanes : (f + 1) * lanes
            ]


def update_kernel(y_ref, p_ref, d_ref, ny_ref, np_ref):
    rows = y_ref.shape[1]
    for j in range(2):
        ny_ref[j] = y_ref[j] - d_ref[rows_of(rows, j, 4), :]
        np_ref[j] = p_ref[j] - d_ref[rows_of(rows, 2 + j, 4), :]


def swapped(value, distance):
    count = lax.axis_size("space")
    return lax.ppermute(value, "space", [(i, i ^ distance) for i in range(count)])


def mirrored(value, distance):
    spaces = lax.axis_size("space")
    layers = LAYERS
    share = SIDE * SIDE
    devices = layers * share
    pairs = []
    for tm in range(devices):
        other = (tm // share ^ layers // 2) * share + tm % share
        pairs += [(tm * spaces + i, other * spaces + (i ^ distance)) for i in range(spaces)]
    return lax.ppermute(value, ("zl", "y", "x", "space"), pairs)


def shards(state_field, adjoint, target, initial_state, conductivity, reaction):
    steps, width_x, width_y, width_z = state_field.shape
    devices = LAYERS * SIDE * SIDE
    spaces = lax.axis_size("space")
    rows = width_x * width_y
    horizon = steps * devices
    assert steps == 2 and rows == devices and spaces == 4
    f32 = jnp.float32

    def shape(*dims):
        return jax.ShapeDtypeStruct(dims, f32)

    flat = (steps, rows, width_z)
    state_rows = state_field.reshape(flat)
    adjoint_rows = adjoint.reshape(flat)
    packed, material = pl.pallas_call(
        pack_kernel,
        out_shape=(
            shape(rows, 6, 1, width_z),
            shape(2, width_x, width_y, width_z),
        ),
        in_specs=[hbm()] * 5,
        out_specs=(hbm(), vmem()),
        scratch_shapes=[
            pltpu.VMEM((rows, 6, 1, width_z), f32),
            pltpu.SemaphoreType.DMA((8,)),
            pltpu.SemaphoreType.DMA(()),
        ],
        compiler_params=grant,
        name="pack",
    )(
        *(
            pltpu.with_memory_space_constraint(each, pltpu.HBM)
            for each in (
                conductivity,
                reaction,
                state_rows,
                adjoint_rows,
                target.reshape(flat),
            )
        )
    )
    table, twist = solver_table(horizon, devices)
    material_core = swapped(material, 1)
    material_far = mirrored(material, 2)
    by_cell = lax.all_to_all(
        packed.reshape(rows * 3, 2, width_z), LINES, 0, 0, tiled=True
    ).reshape(rows * 6, width_z)
    material_both = swapped(material_far, 1)
    forward, inverse = (halves(jnp.asarray(each)) for each in time_tables(horizon, devices))
    hat = pl.pallas_call(
        forward_kernel,
        out_shape=shape(devices * 8, width_z),
        in_specs=[vmem()] * 4,
        out_specs=vmem(),
        compiler_params=grant,
        name="forward",
    )(*forward, initial_state.reshape(rows, width_z), by_cell)
    grid = (spaces * width_x, 2, width_y // 2, width_z)
    pairs = (spaces * width_x, width_y // 2, width_z)
    faces = pl.pallas_call(
        functools.partial(faces_kernel, devices),
        out_shape=(shape(*grid),) + (shape(*pairs),) * 3 + (shape(*grid),) * 5,
        in_specs=[vmem()] * 5,
        out_specs=(vmem(),) * 9,
        scratch_shapes=[pltpu.VMEM((spaces, 2, width_x, width_y, width_z), f32)],
        compiler_params=grant,
        name="faces",
    )(jnp.asarray(table), material, material_core, material_far, material_both)
    hat, faces = lax.optimization_barrier((hat, faces))
    everyone = ("space",) + LINES
    by_item = lax.all_to_all(hat, everyone, 0, 0, tiled=True)
    solved = pl.pallas_call(
        functools.partial(solve_kernel, devices),
        out_shape=shape(rows * 8, width_z),
        in_specs=[vmem()] * 11,
        out_specs=vmem(),
        scratch_shapes=[pltpu.VMEM(grid, f32)] * 4,
        compiler_params=pltpu.CompilerParams(vmem_limit_bytes=8 * 1024 * 1024),
        name="solve",
    )(jnp.asarray(table), *faces, by_item)
    by_row = lax.all_to_all(solved, everyone, 0, 0, tiled=True)
    delta = pl.pallas_call(
        inverse_kernel,
        out_shape=shape(devices * 4, width_z),
        in_specs=[vmem()] * 4,
        out_specs=vmem(),
        compiler_params=grant,
        name="inverse",
    )(*inverse, jnp.asarray(twist_block(twist)), by_row)
    by_time = lax.all_to_all(delta, LINES, 0, 0, tiled=True)
    new_state, new_adjoint = pl.pallas_call(
        update_kernel,
        out_shape=(shape(*flat), shape(*flat)),
        in_specs=[vmem()] * 3,
        out_specs=(vmem(), vmem()),
        compiler_params=grant,
        name="update",
    )(state_rows, adjoint_rows, by_time)
    return new_state.reshape(state_field.shape), new_adjoint.reshape(adjoint.shape)


def solution(mesh):
    fine = Mesh(
        mesh.devices.reshape(LAYERS, SIDE, SIDE, mesh.devices.shape[1]),
        ("zl", "y", "x", "space"),
    )
    time = ("zl", "y", "x")
    in_specs = (
        P(time, "space", None, None),
        P(time, "space", None, None),
        P(time, "space", None, None),
        P("space", None, None),
        P("space", None, None),
        P("space", None, None),
    )
    out_specs = (P(time, "space", None, None), P(time, "space", None, None))
    return jax.shard_map(
        shards, mesh=fine, in_specs=in_specs, out_specs=out_specs, check_vma=False
    )
```
